32 devices in a mesh: qa: 4 (over y, x), qb: 8 (over z, core).
Axes of the slice: x: 2, y: 2, z: 4, core: 2. Of those that a mesh axis runs over, the one named last changes fastest.
Arguments:
- amplitudes: float32 [2, 2097152], P(None, ('qa', 'qb')), may hold values from -6 to 6
- gate_blocks: float32 [4, 6, 2, 128, 128], replicated, may hold values from -0.375 to 0.375
- phase_low: float32 [4, 256], replicated, may hold values from -3.140625 to 3.140625
- phase_high: float32 [4, 256], replicated, may hold values from -3.140625 to 3.140625
- phase_global: float32 [4, 4, 8], P(None, 'qa', 'qb'), may hold values from -3.140625 to 3.140625
Outputs:
- final_state: float32 [2, 2097152], P(None, ('qa', 'qb'))
The draws below stay inside these ranges and needn't reach their ends.
All inputs are finite; a program needn't handle non-finite values.
Results may differ from the reference program's by a relative error of at most 0.00011.
Values sent between devices are 32-bit elements; how exact they have to be, the bound alone decides.
No kernel may reach another device: no remote copies, remote signals or barrier semaphores. Data moves between devices by JAX's collectives and lax.ppermute only.
A program may use at most 64 MiB of HBM per device.

```python
import jax
import jax.numpy as jnp
from jax import lax

GQ = 7
SEG = 4
GATES = 6
LOWQ = 8
HIGHQ = 8
AMPS = 2097152
N_QA = 4
N_QB = 8


def shard_levels(stream_key, shape, shards, smallest, largest):
    gain, own = 1.0, jax.random.fold_in(stream_key, 6)
    for axis_at, blocks in shards:
        heights = jnp.exp(jax.random.uniform(jax.random.fold_in(own, axis_at), (blocks,), jnp.float32, smallest / len(shards), largest / len(shards)))
        gain = gain * jnp.repeat(heights, shape[axis_at] // blocks).reshape([-1 if axis == axis_at else 1 for axis in range(len(shape))])
    return gain


def normal_values(own_key, dims, scale, reach, split=(), kind=jnp.bfloat16):
    loudness = shard_levels(own_key, dims, split, -0.22, 0.18) if split else 1.0
    entries = jax.random.normal(own_key, dims, jnp.float32) * scale * loudness
    return jnp.minimum(jnp.maximum(entries, -reach), reach).astype(kind)


def setup_inputs(seed: int = 0) -> dict:
    keys = jax.random.split(jax.random.key(seed), 6)
    amplitudes = normal_values(keys[0], (2, AMPS), 1.0, 6.0, ((1, 32),), jnp.float32)
    gate_blocks = normal_values(keys[1], (SEG, GATES, 2, 2 ** GQ, 2 ** GQ), (2 * 2 ** GQ) ** -0.5, 0.375, (), jnp.float32)
    phase_low = jnp.clip(jax.random.uniform(keys[2], (SEG, 2 ** LOWQ), jnp.float32, -3.140625, 3.140625), -3.140625, 3.140625)
    phase_high = jnp.clip(jax.random.uniform(keys[3], (SEG, 2 ** HIGHQ), jnp.float32, -3.140625, 3.140625), -3.140625, 3.140625)
    phase_global = jnp.clip(jax.random.uniform(keys[4], (SEG, N_QA, N_QB), jnp.float32, -3.140625, 3.140625), -3.140625, 3.140625)
    return dict(amplitudes=amplitudes, gate_blocks=gate_blocks, phase_low=phase_low, phase_high=phase_high, phase_global=phase_global)


def gate_part(values, matrix, where):
    if where == 0:
        return jnp.einsum("brj,kj->brk", values, matrix, precision=lax.Precision.HIGHEST)
    if where == 1:
        return jnp.einsum("bhjl,kj->bhkl", values, matrix, precision=lax.Precision.HIGHEST)
    return jnp.einsum("kj,bjr->bkr", matrix, values, precision=lax.Precision.HIGHEST)


def apply_gate(state, matrix, where):
    width = matrix.shape[-1]
    blocks, cells = state.shape[1], state.shape[2]
    if where == 0:
        shape = (blocks, cells // width, width)
    elif where == 1:
        shape = (blocks, cells // (width * width), width, width)
    else:
        shape = (blocks, width, cells // width)
    real = state[0].reshape(shape)
    imag = state[1].reshape(shape)
    out_real = gate_part(real, matrix[0], where) - gate_part(imag, matrix[1], where)
    out_imag = gate_part(real, matrix[1], where) + gate_part(imag, matrix[0], where)
    return jnp.stack([out_real.reshape(blocks, cells), out_imag.reshape(blocks, cells)])


def apply_phase(state, low_angles, high_angles, global_angles):
    local = (high_angles[:, None] + low_angles[None, :]).reshape(-1)
    theta = global_angles.reshape(-1, 1) + local[None, :]
    cosine = jnp.cos(theta)
    sine = jnp.sin(theta)
    return jnp.stack([state[0] * cosine - state[1] * sine, state[0] * sine + state[1] * cosine])


def reference(amplitudes, gate_blocks, phase_low, phase_high, phase_global):
    cells = amplitudes.shape[1] // (N_QA * N_QB)
    state = amplitudes.reshape(2, N_QA * N_QB, cells)
    for segment in range(SEG):
        for gate in range(GATES):
            state = apply_gate(state, gate_blocks[segment, gate], gate % 3)
        state = apply_phase(state, phase_low[segment], phase_high[segment], phase_global[segment])
        if segment == 0 or segment == 2:
            grid = state.reshape(2, N_QA, N_QB, N_QA, cells // N_QA)
            state = jnp.transpose(grid, (0, 3, 2, 1, 4)).reshape(2, N_QA * N_QB, cells)
        elif segment == 1:
            grid = state.reshape(2, N_QA, N_QB, N_QB, cells // N_QB)
            state = jnp.transpose(grid, (0, 1, 3, 2, 4)).reshape(2, N_QA * N_QB, cells)
    return state.reshape(2, N_QA * N_QB * cells)
```

```python
import functools

import jax
import jax.numpy as jnp
from jax import lax
from jax.experimental import pallas as pl
from jax.experimental.pallas import tpu as pltpu
from jax.sharding import PartitionSpec as P

F32 = jnp.float32
BF16 = jnp.bfloat16
SLAB = 16


def split(x):
    high = x.astype(BF16)
    return high, (x - high.astype(F32)).astype(BF16)


def dot(a, b):
    return jnp.dot(a, b, preferred_element_type=F32)


def dot3(ah, al, bh, bl):
    return dot(ah, bh) + (dot(al, bh) + dot(ah, bl))


def block_of(real, imag):
    top = jnp.concatenate([real, -imag], axis=1)
    low = jnp.concatenate([imag, real], axis=1)
    return jnp.concatenate([top, low], axis=0)


def inner_order(q, width, spect):
    group = SLAB * spect
    return (q // group) * group + (q % spect) * SLAB + (q % group) // spect


def one_hot(rows, cols, test):
    r = lax.broadcasted_iota(jnp.int32, (rows, cols), 0)
    c = lax.broadcasted_iota(jnp.int32, (rows, cols), 1)
    return jnp.where(test(r, c), 1.0, 0.0).astype(BF16)


def middle_weight(gate, spect, interleaved=False):
    width = gate.shape[-1]
    left = one_hot(width, width, lambda r, c: r == inner_order(c, width, spect))
    out = []
    for parts in zip(split(gate[0]), split(gate[1])):
        real = dot(left, parts[0]).astype(BF16)
        imag = dot(left, parts[1]).astype(BF16)
        if interleaved:
            right = one_hot(
                2 * width, 2 * width, lambda r, c: c == (r % width) * 2 + r // width
            )
            out.append(dot(block_of(real, imag), right).astype(BF16))
        else:
            right = one_hot(width, width, lambda r, c: c == inner_order(r, width, spect))
            real = dot(real, right).astype(BF16)
            imag = dot(imag, right).astype(BF16)
            out.append(block_of(real, imag))
    return out


def upper_weight(gate, cosine=None, sine=None):
    real, imag = gate[0], gate[1]
    if cosine is not None:
        real, imag = real * cosine - imag * sine, real * sine + imag * cosine
    return [block_of(r, i) for r, i in zip(split(real), split(imag))]


def lower_weight(first, second):
    width = first.shape[-1]
    lh, ll = split(jnp.concatenate([second[0], second[1]], axis=1))
    top = jnp.concatenate([first[0], first[1]], axis=1)
    low = jnp.concatenate([-first[1], first[0]], axis=1)
    rh, rl = split(jnp.concatenate([top, low], axis=0))
    joined = dot3(lh, ll, rh, rl)
    real, imag = joined[:, :width].T, joined[:, width:].T
    return [block_of(r, -i) for r, i in zip(split(real), split(imag))]


def weights(gates, spect, cosine, sine, first):
    return [
        lower_weight(gates[0], gates[3]),
        middle_weight(gates[1], spect, first),
        upper_weight(gates[2]),
        middle_weight(gates[4], spect),
        upper_weight(gates[5], cosine, sine),
    ]


def apply_lower(xh, xl, w):
    u, v, j, _, k, l = xh.shape
    rows = u * v * j * k

    def flat(x):
        return jnp.concatenate(
            [x[:, :, :, 0].reshape(rows, l), x[:, :, :, 1].reshape(rows, l)], axis=1
        )

    y = dot3(flat(xh), flat(xl), w[0], w[1])
    return y[:, :l].reshape(u, v, j, k, l), y[:, l:].reshape(u, v, j, k, l)


def columns(x, axis, at):
    u, v, j, _, k, l = x.shape
    out = []
    for one in at:
        part = x[one] if axis == 0 else x[:, :, one]
        a, b = part.shape[0], part.shape[1]
        real, imag = part[:, :, 0], part[:, :, 1]
        out.append(
            jnp.concatenate([real.reshape(a * b * k, l), imag.reshape(a * b * k, l)], axis=0)
        )
    return jnp.concatenate(out, axis=1)


def apply_rows(hi_ref, lo_ref, w, axis, done):
    u, v, j, _, k, l = hi_ref.shape
    count, inner = (u, (v, j)) if axis == 0 else (j, (u, v))
    half = inner[0] * inner[1] * k
    for at in range(0, count, 2):
        pair = (at, at + 1)

        def take(ref):
            out = []
            for one in pair:
                part = ref[one] if axis == 0 else ref[:, :, one]
                out.append(
                    jnp.concatenate(
                        [part[:, :, 0].reshape(half, l), part[:, :, 1].reshape(half, l)], axis=0
                    )
                )
            return jnp.concatenate(out, axis=1)

        y = dot3(w[0], w[1], take(hi_ref), take(lo_ref))
        for n, one in enumerate(pair):
            part = y[:, n * l : (n + 1) * l]
            done(one, part[:half].reshape(*inner, k, l), part[half:].reshape(*inner, k, l))


def keeper(hi_ref, lo_ref, axis):
    def keep(one, real, imag):
        for ri, value in ((0, real), (1, imag)):
            high, low = split(value)
            if axis == 0:
                hi_ref[one, :, :, ri] = high
                lo_ref[one, :, :, ri] = low
            else:
                hi_ref[:, :, one, ri] = high
                lo_ref[:, :, one, ri] = low

    return keep


def lower_in_place(hi_ref, lo_ref, w):
    real, imag = apply_lower(hi_ref[...], lo_ref[...], w)
    for ri, value in ((0, real), (1, imag)):
        high, low = split(value)
        hi_ref[:, :, :, ri] = high
        lo_ref[:, :, :, ri] = low


def first_kernel(spect, scalar_ref, x_ref, gate_ref, o_ref, hi_ref, lo_ref):
    u, v, j, _, k, l = hi_ref.shape
    w = weights(gate_ref[0], spect, scalar_ref[0, 0], scalar_ref[1, 0], True)
    block = 2 * v * j * k
    keep = keeper(hi_ref, lo_ref, 0)
    for at in range(0, u, 2):
        both = jnp.concatenate(
            [x_ref[at * block : (at + 1) * block], x_ref[(at + 1) * block : (at + 2) * block]],
            axis=1,
        )
        xh, xl = split(both)
        y = dot3(w[1][0], w[1][1], xh, xl)
        for n in range(2):
            part = y[:, n * l : (n + 1) * l]
            keep(
                at + n,
                part[: block // 2].reshape(v, j, k, l),
                part[block // 2 :].reshape(v, j, k, l),
            )
    apply_rows(hi_ref, lo_ref, w[2], 1, keeper(hi_ref, lo_ref, 1))
    apply_rows(hi_ref, lo_ref, w[3], 0, keeper(hi_ref, lo_ref, 0))
    lower_in_place(hi_ref, lo_ref, w[0])

    def put(one, real, imag):
        o_ref[:, :, one, 0] = real
        o_ref[:, :, one, 1] = imag

    apply_rows(hi_ref, lo_ref, w[4], 1, put)


def prepare_kernel(spect, scalar_ref, gate_ref, w_ref):
    at = pl.program_id(0) + 1
    made = weights(gate_ref[0], spect, scalar_ref[0, at], scalar_ref[1, at], False)
    for n, pair in enumerate(made):
        w_ref[0, n, 0] = pair[0]
        w_ref[0, n, 1] = pair[1]


def later_kernel(last, x_ref, e_ref, w_ref, *rest):
    if last:
        f_ref, o_ref, hi_ref, lo_ref = rest
    else:
        o_ref, hi_ref, lo_ref = rest
    u, v, j, _, k, l = hi_ref.shape
    eu, ev = e_ref.shape[0], e_ref.shape[1]
    for a in range(u):
        for b in range(v):
            c, s = e_ref[a % eu, b % ev, :, 0], e_ref[a % eu, b % ev, :, 1]
            real, imag = x_ref[a, b, :, 0], x_ref[a, b, :, 1]
            for ri, value in ((0, real * c - imag * s), (1, real * s + imag * c)):
                high, low = split(value)
                hi_ref[a, b, :, ri] = high
                lo_ref[a, b, :, ri] = low
    w = [(w_ref[0, n, 0], w_ref[0, n, 1]) for n in range(w_ref.shape[1])]
    lower_in_place(hi_ref, lo_ref, w[0])
    apply_rows(hi_ref, lo_ref, w[1], 0, keeper(hi_ref, lo_ref, 0))
    apply_rows(hi_ref, lo_ref, w[2], 1, keeper(hi_ref, lo_ref, 1))
    apply_rows(hi_ref, lo_ref, w[3], 0, keeper(hi_ref, lo_ref, 0))

    def put(one, real, imag):
        if not last:
            o_ref[:, :, one, 0] = real
            o_ref[:, :, one, 1] = imag
            return
        c, s = f_ref[:, :, one, 0], f_ref[:, :, one, 1]
        both = (real * c - imag * s, real * s + imag * c)
        stride = 2 * j
        for ri, value in enumerate(both):
            for a in range(u):
                for b in range(v):
                    start = (a * v + b) * k * stride + one * 2 + ri
                    o_ref[pl.ds(start, k, stride=stride), :] = value[a, b]

    apply_rows(hi_ref, lo_ref, w[4], 1, put)


def body(amplitudes, gate_blocks, phase_low, phase_high, phase_global):
    cells = amplitudes.shape[1]
    segments, per_segment, _, width, _ = gate_blocks.shape
    spect = cells // (width * width)
    k = SLAB
    v = width // spect // k
    dims = (spect, v, spect, 2, k, width)
    rows = 2 * cells // width
    highs = phase_high.shape[1]
    scalars = phase_global[:, 0, 0]
    scalars = jnp.stack([jnp.cos(scalars), jnp.sin(scalars)])
    smem = pl.BlockSpec(memory_space=pltpu.SMEM)
    vmem = pl.BlockSpec(memory_space=pltpu.VMEM)
    state_scratch = [pltpu.VMEM(dims, BF16), pltpu.VMEM(dims, BF16)]
    gate_shape = (1,) + gate_blocks.shape[1:]
    flops = 10 * 8 * cells * width

    x = amplitudes.reshape(2, cells // width, width).transpose(1, 0, 2).reshape(rows, width)
    state = pl.pallas_call(
        functools.partial(first_kernel, spect),
        out_shape=jax.ShapeDtypeStruct(dims, F32),
        grid=(1,),
        in_specs=[
            smem,
            pl.BlockSpec((rows, width), lambda i: (0, 0)),
            pl.BlockSpec(gate_shape, lambda i: (0, 0, 0, 0, 0)),
        ],
        out_specs=pl.BlockSpec(dims, lambda i: (0,) * 6),
        scratch_shapes=state_scratch,
        cost_estimate=pl.CostEstimate(flops=flops, bytes_accessed=16 * cells, transcendentals=0),
    )(scalars, x, gate_blocks)

    made = pl.pallas_call(
        functools.partial(prepare_kernel, spect),
        out_shape=jax.ShapeDtypeStruct((segments - 1, 5, 2, 2 * width, 2 * width), BF16),
        grid=(segments - 1,),
        in_specs=[smem, pl.BlockSpec(gate_shape, lambda i: (i + 1, 0, 0, 0, 0))],
        out_specs=pl.BlockSpec((1, 5, 2, 2 * width, 2 * width), lambda i: (i, 0, 0, 0, 0)),
        cost_estimate=pl.CostEstimate(
            flops=flops, bytes_accessed=16 * cells, transcendentals=0
        ),
    )(scalars, gate_blocks)

    def table(segment, count, index):
        high = phase_high[segment]
        if count > 1:
            high = lax.dynamic_slice_in_dim(high, index * (highs // count), highs // count)
            few = max(highs // count, k * (highs // (spect * v * k)))
            high = jnp.tile(high, few // (highs // count))
        upper = high.shape[0] // (k * 2)
        eu, ev = (upper // v, v) if upper >= v else (1, 1)
        low = phase_low[segment].reshape(2, width)
        high = high.reshape(eu, ev, k, spect // 2).transpose(0, 1, 3, 2)

        def grid(a, b):
            return a[:, :, :, None, :, None] * b[None, None, None, :, None, :]

        ch, sh, cl, sl = jnp.cos(high), jnp.sin(high), jnp.cos(low), jnp.sin(low)
        cosine = grid(ch, cl) - grid(sh, sl)
        sine = grid(sh, cl) + grid(ch, sl)
        both = jnp.stack([cosine, sine], axis=4)
        return both.reshape(eu, ev, spect, 2, k, width)

    def exchange(value, name):
        count = lax.axis_size(name)
        tops = spect * v
        if count <= tops:
            blocks = value.reshape(count, rows // count, width)
            moved = lax.all_to_all(blocks, name, split_axis=0, concat_axis=0, tiled=True)
            return moved.reshape(dims)
        more = count // tops
        blocks = value.reshape(tops, spect * 2, more, k // more, width)
        blocks = blocks.transpose(0, 2, 1, 3, 4).reshape(count, rows // count, width)
        moved = lax.all_to_all(blocks, name, split_axis=0, concat_axis=0, tiled=True)
        moved = moved.reshape(tops, more, spect * 2, k // more, width)
        return moved.transpose(0, 2, 1, 3, 4).reshape(dims)

    final = table(segments - 1, 1, 0)
    for segment in range(1, segments):
        name = "qb" if segment == 2 else "qa"
        state = exchange(state, name)
        entry = table(segment - 1, lax.axis_size(name), lax.axis_index(name))
        last = segment == segments - 1
        extra = [final] if last else []
        out = (rows, width) if last else dims
        state = pl.pallas_call(
            functools.partial(later_kernel, last),
            out_shape=jax.ShapeDtypeStruct(out, F32),
            grid=(1,),
            in_specs=[
                pl.BlockSpec(dims, lambda i: (0,) * 6),
                pl.BlockSpec(entry.shape, lambda i: (0,) * 6),
                pl.BlockSpec(
                    (1, 5, 2, 2 * width, 2 * width), lambda i, s=segment: (s - 1, 0, 0, 0, 0)
                ),
            ]
            + [pl.BlockSpec(f.shape, lambda i: (0,) * 6) for f in extra],
            out_specs=pl.BlockSpec(out, lambda i, n=len(out): (0,) * n),
            scratch_shapes=state_scratch,
            cost_estimate=pl.CostEstimate(
                flops=flops, bytes_accessed=24 * cells, transcendentals=0
            ),
        )(state, entry, made, *extra)
    return state.reshape(cells // width, 2, width).transpose(1, 0, 2).reshape(2, cells)


def solution(mesh):
    return jax.shard_map(
        body,
        mesh=mesh,
        in_specs=(P(None, ("qa", "qb")), P(), P(), P(), P(None, "qa", "qb")),
        out_specs=P(None, ("qa", "qb")),
        check_vma=False,
    )
```

```python
import functools

import jax
import jax.numpy as jnp
from jax import lax
from jax.experimental import pallas as pl
from jax.experimental.pallas import tpu as pltpu
from jax.sharding import PartitionSpec as P

F32 = jnp.float32
BF16 = jnp.bfloat16
SLAB = 16
VMEM_LIMIT = 16 << 20


def split(x):
    high = x.astype(BF16)
    return high, (x - high.astype(F32)).astype(BF16)


def dot(a, b):
    return jnp.dot(a, b, preferred_element_type=F32)


def dot3(ah, al, bh, bl):
    return dot(ah, bh) + (dot(al, bh) + dot(ah, bl))


def block_of(real, imag):
    top = jnp.concatenate([real, -imag], axis=1)
    low = jnp.concatenate([imag, real], axis=1)
    return jnp.concatenate([top, low], axis=0)


def inner_order(q, width, spect):
    group = SLAB * spect
    return (q // group) * group + (q % spect) * SLAB + (q % group) // spect


def one_hot(rows, cols, test):
    r = lax.broadcasted_iota(jnp.int32, (rows, cols), 0)
    c = lax.broadcasted_iota(jnp.int32, (rows, cols), 1)
    return jnp.where(test(r, c), 1.0, 0.0).astype(BF16)


def middle_weight(gate, spect, interleaved=False):
    width = gate.shape[-1]
    left = one_hot(width, width, lambda r, c: r == inner_order(c, width, spect))
    out = []
    for parts in zip(split(gate[0]), split(gate[1])):
        real = dot(left, parts[0]).astype(BF16)
        imag = dot(left, parts[1]).astype(BF16)
        if interleaved:
            right = one_hot(
                2 * width, 2 * width, lambda r, c: c == (r % width) * 2 + r // width
            )
            out.append(dot(block_of(real, imag), right).astype(BF16))
        else:
            right = one_hot(width, width, lambda r, c: c == inner_order(r, width, spect))
            real = dot(real, right).astype(BF16)
            imag = dot(imag, right).astype(BF16)
            out.append(block_of(real, imag))
    return out


def upper_weight(gate, cosine=None, sine=None):
    real, imag = gate[0], gate[1]
    if cosine is not None:
        real, imag = real * cosine - imag * sine, real * sine + imag * cosine
    return [block_of(r, i) for r, i in zip(split(real), split(imag))]


def lower_weight(first, second):
    width = first.shape[-1]
    lh, ll = split(jnp.concatenate([second[0], second[1]], axis=1))
    top = jnp.concatenate([first[0], first[1]], axis=1)
    low = jnp.concatenate([-first[1], first[0]], axis=1)
    rh, rl = split(jnp.concatenate([top, low], axis=0))
    joined = dot3(lh, ll, rh, rl)
    real, imag = joined[:, :width].T, joined[:, width:].T
    return [block_of(r, -i) for r, i in zip(split(real), split(imag))]


def put_rows(w_ref, n, pair, group, mask):
    half = pair[0].shape[0] // 2
    for p, value in enumerate(pair):
        for ri in range(2):
            for g in range(half // group):
                start = pl.multiple_of(ri * half + (g ^ mask) * group, group)
                at = ri * half + g * group
                w_ref[n, p, pl.ds(start, group), :] = value[at : at + group]


def put(w_ref, n, pair):
    w_ref[n, 0] = pair[0]
    w_ref[n, 1] = pair[1]


def rotation(ref, segment, width):
    theta = jnp.broadcast_to(ref[segment], (1, width))
    return jnp.cos(theta), jnp.sin(theta)


def apply_lower(xh, xl, w):
    u, v, j, _, k, l = xh.shape
    rows = u * v * j * k

    def flat(x):
        return jnp.concatenate(
            [x[:, :, :, 0].reshape(rows, l), x[:, :, :, 1].reshape(rows, l)], axis=1
        )

    y = dot3(flat(xh), flat(xl), w[0], w[1])
    return y[:, :l].reshape(u, v, j, k, l), y[:, l:].reshape(u, v, j, k, l)


def lower_in_place(hi_ref, lo_ref, w):
    real, imag = apply_lower(hi_ref[...], lo_ref[...], w)
    for ri, value in ((0, real), (1, imag)):
        high, low = split(value)
        hi_ref[:, :, :, ri] = high
        lo_ref[:, :, :, ri] = low


def apply_rows(hi_ref, lo_ref, w, axis, done):
    u, v, j, _, k, l = hi_ref.shape
    count, inner = (u, (v, j)) if axis == 0 else (j, (u, v))
    half = inner[0] * inner[1] * k
    for at in range(0, count, 2):
        pair = (at, at + 1)

        def take(ref):
            out = []
            for one in pair:
                part = ref[one] if axis == 0 else ref[:, :, one]
                out.append(
                    jnp.concatenate(
                        [part[:, :, 0].reshape(half, l), part[:, :, 1].reshape(half, l)], axis=0
                    )
                )
            return jnp.concatenate(out, axis=1)

        y = dot3(w[0], w[1], take(hi_ref), take(lo_ref))
        for n, one in enumerate(pair):
            part = y[:, n * l : (n + 1) * l]
            done(one, part[:half].reshape(*inner, k, l), part[half:].reshape(*inner, k, l))


def keeper(hi_ref, lo_ref, axis):
    def keep(one, real, imag):
        for ri, value in ((0, real), (1, imag)):
            high, low = split(value)
            if axis == 0:
                hi_ref[one, :, :, ri] = high
                lo_ref[one, :, :, ri] = low
            else:
                hi_ref[:, :, one, ri] = high
                lo_ref[:, :, one, ri] = low

    return keep


def mask_of(name, count, dims):
    if name is None:
        return 0
    return lax.axis_index(name) * (dims[0] * dims[1] // count)


def sender(outs, order, dims):
    tops = dims[0] * dims[1]
    few = tops // len(outs)

    def put_out(one, real, imag):
        for ri, value in ((0, real), (1, imag)):
            value = value.reshape(len(outs), few, *value.shape[2:])
            for ref, place in zip(outs, order):
                ref[:, one, ri] = value[place]

    return put_out


def load_gates(gate_hbm, segment, gate_ref, sems):
    return [
        pltpu.make_async_copy(gate_hbm.at[segment, g], gate_ref.at[g], sems.at[g])
        for g in range(gate_ref.shape[0])
    ]


def first_kernel(spect, name, count, order, x_hbm, gate_hbm, angle_hbm, *rest):
    outs = rest[: len(order)]
    hi_ref, lo_ref, x_ref, gate_ref, angle_ref, w_ref, gate_sem, x_sem = rest[len(order) :]
    u, v, j, _, k, l = hi_ref.shape
    gates = load_gates(gate_hbm, 0, gate_ref, gate_sem)
    block = 2 * v * j * k
    parts = [
        pltpu.make_async_copy(
            x_hbm.at[pl.ds(a * block, block)], x_ref.at[pl.ds(a * block, block)], x_sem.at[a]
        )
        for a in range(u)
    ]
    angle = pltpu.make_async_copy(angle_hbm, angle_ref, x_sem.at[u])
    gates[1].start()
    for part in parts:
        part.start()
    for g in (2, 4, 0, 3, 5):
        gates[g].start()
    angle.start()
    gates[1].wait()
    first = middle_weight(gate_ref[1], spect, True)
    keep = keeper(hi_ref, lo_ref, 0)
    for at in range(0, u, 2):
        parts[at].wait()
        parts[at + 1].wait()
        both = jnp.concatenate(
            [x_ref[at * block : (at + 1) * block], x_ref[(at + 1) * block : (at + 2) * block]],
            axis=1,
        )
        xh, xl = split(both)
        y = dot3(first[0], first[1], xh, xl)
        for n in range(2):
            part = y[:, n * l : (n + 1) * l]
            keep(
                at + n,
                part[: block // 2].reshape(v, j, k, l),
                part[block // 2 :].reshape(v, j, k, l),
            )
    gates[2].wait()
    apply_rows(hi_ref, lo_ref, upper_weight(gate_ref[2]), 1, keeper(hi_ref, lo_ref, 1))
    gates[4].wait()
    apply_rows(hi_ref, lo_ref, middle_weight(gate_ref[4], spect), 0, keeper(hi_ref, lo_ref, 0))
    gates[0].wait()
    gates[3].wait()
    lower_in_place(hi_ref, lo_ref, lower_weight(gate_ref[0], gate_ref[3]))
    gates[5].wait()
    angle.wait()
    cosine, sine = rotation(angle_ref, 0, l)
    put_rows(
        w_ref, 0, upper_weight(gate_ref[5], cosine, sine), k, mask_of(name, count, (u, v))
    )
    apply_rows(hi_ref, lo_ref, (w_ref[0, 0], w_ref[0, 1]), 1, sender(outs, order, (u, v)))


def prepare_kernel(spect, segment, name, count, gate_hbm, angle_hbm, *rest):
    w_ref, gate_ref, angle_ref, gate_sem, angle_sem = rest[-5:]
    gates = load_gates(gate_hbm, segment, gate_ref, gate_sem)
    angle = pltpu.make_async_copy(angle_hbm, angle_ref, angle_sem)
    for copy in gates + [angle]:
        copy.start()
    for copy in gates + [angle]:
        copy.wait()
    width = gate_ref.shape[-1]
    cosine, sine = rotation(angle_ref, segment, width)
    put(w_ref, 0, lower_weight(gate_ref[0], gate_ref[3]))
    put(w_ref, 1, middle_weight(gate_ref[1], spect))
    put(w_ref, 2, upper_weight(gate_ref[2]))
    put(w_ref, 3, middle_weight(gate_ref[4], spect))
    last = upper_weight(gate_ref[5], cosine, sine)
    if name is None:
        put(w_ref, 4, last)
    else:
        tops = (spect, width // spect // SLAB)
        put_rows(w_ref, 4, last, SLAB, mask_of(name, count, tops))


def later_kernel(name, count, order, out_order, last, *refs):
    slots, (e_ref, w_ref), rest = refs[: len(order)], refs[len(order) : len(order) + 2], refs[
        len(order) + 2 :
    ]
    if last:
        f_ref, o_hbm, hi_ref, lo_ref, o_ref, o_sem = rest
    else:
        outs, (hi_ref, lo_ref) = rest[:-2], rest[-2:]
    u, v, j, _, k, l = hi_ref.shape
    mask = mask_of(name, count, (u, v))
    few = u * v // len(order)
    for ref, place in zip(slots, order):
        for n in range(few):
            at = (place * few + n) ^ mask
            a, b = at // v, at % v
            ev = n % e_ref.shape[0]
            c, s = e_ref[ev, :, 0], e_ref[ev, :, 1]
            real, imag = ref[n, :, 0], ref[n, :, 1]
            for ri, value in ((0, real * c - imag * s), (1, real * s + imag * c)):
                high, low = split(value)
                hi_ref[a, b, :, ri] = high
                lo_ref[a, b, :, ri] = low
    w = [(w_ref[n, 0], w_ref[n, 1]) for n in range(w_ref.shape[0])]
    lower_in_place(hi_ref, lo_ref, w[0])
    apply_rows(hi_ref, lo_ref, w[1], 0, keeper(hi_ref, lo_ref, 0))
    apply_rows(hi_ref, lo_ref, w[2], 1, keeper(hi_ref, lo_ref, 1))
    apply_rows(hi_ref, lo_ref, w[3], 0, keeper(hi_ref, lo_ref, 0))
    if not last:
        apply_rows(hi_ref, lo_ref, w[4], 1, sender(outs, out_order, (u, v)))
        return

    stride = 2 * j

    def finish(one, real, imag):
        c, s = f_ref[:, :, one, 0], f_ref[:, :, one, 1]
        both = (real * c - imag * s, real * s + imag * c)
        for ri, value in enumerate(both):
            for a in range(u):
                for b in range(v):
                    start = (a * v + b) * k * stride + one * 2 + ri
                    o_ref[pl.ds(start, k, stride=stride), :] = value[a, b]

    apply_rows(hi_ref, lo_ref, w[4], 1, finish)
    block = v * k * stride
    copies = [
        pltpu.make_async_copy(
            o_ref.at[pl.ds(a * block, block)], o_hbm.at[pl.ds(a * block, block)], o_sem.at[a]
        )
        for a in range(u)
    ]
    for copy in copies:
        copy.start()
    for copy in copies:
        copy.wait()


ORDERS = {4: (1, 2, 3, 0), 8: (6, 4, 7, 5, 2, 3, 1, 0)}


def body(amplitudes, gate_blocks, phase_low, phase_high, phase_global):
    cells = amplitudes.shape[1]
    segments, per_segment, _, width, _ = gate_blocks.shape
    spect = cells // (width * width)
    k = SLAB
    v = width // spect // k
    dims = (spect, v, spect, 2, k, width)
    tops = spect * v
    rows = 2 * cells // width
    highs = phase_high.shape[1]
    vmem = pl.BlockSpec(memory_space=pltpu.VMEM)
    anywhere = pl.BlockSpec(memory_space=pl.ANY)
    hbm = pl.BlockSpec(memory_space=pltpu.HBM)
    state_scratch = [pltpu.VMEM(dims, BF16), pltpu.VMEM(dims, BF16)]
    gate_scratch = [
        pltpu.VMEM(gate_blocks.shape[1:], F32),
        pltpu.VMEM(phase_global.shape, F32),
    ]
    in_hbm = functools.partial(pltpu.with_memory_space_constraint, memory_space=pltpu.HBM)
    gates, angles = in_hbm(gate_blocks), in_hbm(phase_global)
    params = pltpu.CompilerParams(vmem_limit_bytes=VMEM_LIMIT)

    def cost(scale):
        return pl.CostEstimate(
            flops=int(40 * cells * width * scale),
            bytes_accessed=int(8 * cells * scale),
            transcendentals=0,
        )

    def plan(segment):
        name = "qb" if segment == 1 else "qa"
        count = lax.axis_size(name)
        if count in ORDERS and count <= tops:
            return name, count, name, ORDERS[count]
        return name, count, None, tuple(range(tops))

    def slots_of(order):
        shape = (tops // len(order),) + dims[2:]
        return [jax.ShapeDtypeStruct(shape, F32) for _ in order]

    def exchange(values, segment):
        name, count, mask, order = plan(segment)
        if mask is not None:
            return [
                lax.ppermute(value, name, [(i, i ^ place) for i in range(count)])
                if place
                else value
                for value, place in zip(values, order)
            ]
        value = jnp.concatenate(values, axis=0)
        more = max(count // tops, 1)
        blocks = value.reshape(tops, spect * 2, more, k // more, width)
        blocks = blocks.transpose(0, 2, 1, 3, 4).reshape(count, rows // count, width)
        moved = lax.all_to_all(blocks, name, split_axis=0, concat_axis=0, tiled=True)
        moved = moved.reshape(tops, more, spect * 2, k // more, width)
        moved = moved.transpose(0, 2, 1, 3, 4).reshape((tops, 1) + dims[2:])
        return [moved[i] for i in range(tops)]

    def table(high, low, count, index):
        if count > 1:
            high = lax.dynamic_slice_in_dim(high, index * (highs // count), highs // count)
            few = max(highs // count, highs // tops)
            high = jnp.tile(high, few // (highs // count))
        upper = high.shape[0] // (highs // tops)
        low = low.reshape(2, width)
        high = high.reshape(upper, k, spect // 2).transpose(0, 2, 1)

        def grid(a, b):
            return a[:, :, None, :, None] * b[None, None, :, None, :]

        ch, sh, cl, sl = jnp.cos(high), jnp.sin(high), jnp.cos(low), jnp.sin(low)
        cosine = grid(ch, cl) - grid(sh, sl)
        sine = grid(sh, cl) + grid(ch, sl)
        both = jnp.stack([cosine, sine], axis=3)
        return both.reshape(upper, spect, 2, k, width)

    x = amplitudes.reshape(2, cells // width, width).transpose(1, 0, 2).reshape(rows, width)
    name, count, mask, order = plan(0)
    state = pl.pallas_call(
        functools.partial(first_kernel, spect, mask, count, order),
        out_shape=slots_of(order),
        in_specs=[hbm] * 3,
        out_specs=[vmem] * len(order),
        scratch_shapes=state_scratch
        + [pltpu.VMEM((rows, width), F32)]
        + gate_scratch
        + [
            pltpu.VMEM((1, 2, 2 * width, 2 * width), BF16),
            pltpu.SemaphoreType.DMA((per_segment,)),
            pltpu.SemaphoreType.DMA((spect + 1,)),
        ],
        compiler_params=params,
        cost_estimate=cost(1),
    )(in_hbm(x), gates, angles)

    w_shape = (per_segment - 1, 2, 2 * width, 2 * width)
    for segment in range(1, segments):
        before = state[0]
        in_name, in_count, in_mask, in_order = plan(segment - 1)
        last = segment == segments - 1
        _, out_count, out_mask, out_order = (None,) * 4 if last else plan(segment)
        made = pl.pallas_call(
            functools.partial(prepare_kernel, spect, segment, out_mask, out_count),
            out_shape=jax.ShapeDtypeStruct(w_shape, BF16),
            in_specs=[hbm, hbm, anywhere],
            out_specs=vmem,
            scratch_shapes=gate_scratch
            + [pltpu.SemaphoreType.DMA((per_segment,)), pltpu.SemaphoreType.DMA(())],
            compiler_params=params,
            cost_estimate=cost(1),
        )(gates, angles, before)
        high, low, tail_high, tail_low, _ = lax.optimization_barrier(
            (phase_high[segment - 1], phase_low[segment - 1], phase_high[segment],
             phase_low[segment], before)
        )
        entry = table(high, low, in_count, lax.axis_index(in_name))
        extra = []
        if last:
            extra = [table(tail_high, tail_low, 1, 0).reshape(dims)]
        state = exchange(state, segment - 1)
        state = pl.pallas_call(
            functools.partial(later_kernel, in_mask, in_count, in_order, out_order, last),
            out_shape=jax.ShapeDtypeStruct((rows, width), F32) if last else slots_of(out_order),
            in_specs=[vmem] * (len(in_order) + 2 + len(extra)),
            out_specs=hbm if last else [vmem] * len(out_order),
            scratch_shapes=state_scratch
            + (
                [pltpu.VMEM((rows, width), F32), pltpu.SemaphoreType.DMA((spect,))]
                if last
                else []
            ),
            compiler_params=params,
            cost_estimate=cost(1),
        )(*state, entry, made, *extra)
    return state.reshape(cells // width, 2, width).transpose(1, 0, 2).reshape(2, cells)


def solution(mesh):
    return jax.shard_map(
        body,
        mesh=mesh,
        in_specs=(P(None, ("qa", "qb")), P(), P(), P(), P(None, "qa", "qb")),
        out_specs=P(None, ("qa", "qb")),
        check_vma=False,
    )
```

```python
import functools

import jax
import jax.numpy as jnp
from jax import lax
from jax.experimental import pallas as pl
from jax.experimental.pallas import tpu as pltpu
from jax.sharding import PartitionSpec as P

F32 = jnp.float32
BF16 = jnp.bfloat16
SLAB = 16
VMEM_LIMIT = 16 << 20


def split(x):
    high = x.astype(BF16)
    return high, (x - high.astype(F32)).astype(BF16)


def dot(a, b):
    return jnp.dot(a, b, preferred_element_type=F32)


def dot3(ah, al, bh, bl):
    return dot(ah, bh) + (dot(al, bh) + dot(ah, bl))


def block_of(real, imag):
    top = jnp.concatenate([real, -imag], axis=1)
    low = jnp.concatenate([imag, real], axis=1)
    return jnp.concatenate([top, low], axis=0)


def inner_order(q, width, spect):
    group = SLAB * spect
    return (q // group) * group + (q % spect) * SLAB + (q % group) // spect


def one_hot(rows, cols, test):
    r = lax.broadcasted_iota(jnp.int32, (rows, cols), 0)
    c = lax.broadcasted_iota(jnp.int32, (rows, cols), 1)
    return jnp.where(test(r, c), 1.0, 0.0).astype(BF16)


def rows_inner(ref, width, spect):
    group = SLAB * spect
    return jnp.concatenate(
        [
            ref[pl.ds(top + j, SLAB, stride=spect), :]
            for top in range(0, width, group)
            for j in range(spect)
        ],
        axis=0,
    )


def middle_weight(gate_ref, g, spect, natural=False, flip=0):
    width = gate_ref.shape[-1]
    real = split(rows_inner(gate_ref.at[g, 0], width, spect))
    imag = split(rows_inner(gate_ref.at[g, 1], width, spect))
    if natural:
        return [block_of(r, i) for r, i in zip(real, imag)]
    right = one_hot(width, width, lambda r, c: (c ^ flip) == inner_order(r, width, spect))
    moved = dot(jnp.concatenate([*real, *imag], axis=0), right).astype(BF16)
    part = [moved[n * width : (n + 1) * width] for n in range(4)]
    return [block_of(part[0], part[2]), block_of(part[1], part[3])]


def upper_weight(gate, cosine=None, sine=None):
    real, imag = gate[0], gate[1]
    if cosine is not None:
        real, imag = real * cosine - imag * sine, real * sine + imag * cosine
    return [block_of(r, i) for r, i in zip(split(real), split(imag))]


def lower_weight(first, second):
    width = first.shape[-1]
    lh, ll = split(jnp.concatenate([second[0], second[1]], axis=1))
    top = jnp.concatenate([first[0], first[1]], axis=1)
    low = jnp.concatenate([-first[1], first[0]], axis=1)
    rh, rl = split(jnp.concatenate([top, low], axis=0))
    joined = dot3(lh, ll, rh, rl)
    real, imag = joined[:, :width].T, joined[:, width:].T
    return [block_of(r, -i) for r, i in zip(split(real), split(imag))]


def put_rows(w_ref, n, pair, group, mask):
    half = pair[0].shape[0] // 2
    for p, value in enumerate(pair):
        for ri in range(2):
            for g in range(half // group):
                start = pl.multiple_of(ri * half + (g ^ mask) * group, group)
                at = ri * half + g * group
                w_ref[n, p, pl.ds(start, group), :] = value[at : at + group]


def put(w_ref, n, pair):
    w_ref[n, 0] = pair[0]
    w_ref[n, 1] = pair[1]


def rotation(ref, segment, width):
    theta = jnp.broadcast_to(ref[0:1, segment : segment + 1], (1, width))
    return jnp.cos(theta), jnp.sin(theta)


def lower_rows(xh, xl, w):
    y = dot3(xh, xl, w[0], w[1])
    half = y.shape[1] // 2
    return y[:, :half], y[:, half:]


def side_by_side(x):
    *lead, _, k, l = x.shape
    rows = functools.reduce(lambda m, n: m * n, lead, k)
    x = x.reshape(rows // k, 2, k, l)
    return jnp.concatenate([x[:, 0].reshape(rows, l), x[:, 1].reshape(rows, l)], axis=1)


def row_gate(take, w, l):
    first, second = take(0), take(1)
    y = dot3(
        w[0],
        w[1],
        jnp.concatenate([first[0], second[0]], axis=1),
        jnp.concatenate([first[1], second[1]], axis=1),
    )
    return y[:, :l], y[:, l:]


def apply_rows(hi_ref, lo_ref, w, axis, done, pairs=None):
    u, v, j, _, k, l = hi_ref.shape
    count, inner = (u, (v, j)) if axis == 0 else (j, (u, v))
    half = inner[0] * inner[1] * k

    def column(ref, one):
        part = ref[one] if axis == 0 else ref[:, :, one]
        return jnp.concatenate(
            [part[:, :, 0].reshape(half, l), part[:, :, 1].reshape(half, l)], axis=0
        )

    for at in range(0, count, 2) if pairs is None else pairs:
        parts = row_gate(lambda n: (column(hi_ref, at + n), column(lo_ref, at + n)), w, l)
        for n, part in enumerate(parts):
            done(at + n, part[:half].reshape(*inner, k, l), part[half:].reshape(*inner, k, l))


def keeper(hi_ref, lo_ref, axis):
    def keep(one, real, imag):
        for ri, value in ((0, real), (1, imag)):
            high, low = split(value)
            if axis == 0:
                hi_ref[one, :, :, ri] = high
                lo_ref[one, :, :, ri] = low
            else:
                hi_ref[:, :, one, ri] = high
                lo_ref[:, :, one, ri] = low

    return keep


def mask_of(name, count, dims):
    if name is None:
        return 0
    return lax.axis_index(name) * (dims[0] * dims[1] // count)


def sender(outs, order, dims):
    tops = dims[0] * dims[1]
    few = tops // len(outs)

    def put_out(one, real, imag):
        for ri, value in ((0, real), (1, imag)):
            value = value.reshape(len(outs), few, *value.shape[2:])
            for ref, place in zip(outs, order):
                ref[:, one, ri] = value[place]

    return put_out


def load_gates(gate_hbm, segment, gate_ref, sems):
    return [
        pltpu.make_async_copy(gate_hbm.at[segment, g], gate_ref.at[g], sems.at[g])
        for g in range(gate_ref.shape[0])
    ]


def first_kernel(spect, name, count, order, x_hbm, gate_hbm, angle_hbm, *rest):
    outs = rest[: len(order)]
    hi_ref, lo_ref, x_ref, gate_ref, angle_ref, w_ref, gate_sem, x_sem = rest[len(order) :]
    u, v, j, _, k, l = hi_ref.shape
    gates = load_gates(gate_hbm, 0, gate_ref, gate_sem)
    block = 2 * v * j * k
    parts = [
        pltpu.make_async_copy(
            x_hbm.at[pl.ds(a * block, block)], x_ref.at[pl.ds(a * block, block)], x_sem.at[a]
        )
        for a in range(u)
    ]
    angle = pltpu.make_async_copy(angle_hbm, angle_ref, x_sem.at[u])
    wanted = [gates[1], *parts, gates[2], gates[4], gates[0], gates[3], gates[5], angle]
    for copy in wanted:
        copy.start()
    for copy in wanted:
        copy.wait()
    half = block // 2
    keep = keeper(hi_ref, lo_ref, 0)
    w = middle_weight(gate_ref, 1, spect, True)

    def column(a):
        real = x_ref[pl.ds(a * block, half, stride=2), :]
        imag = x_ref[pl.ds(a * block + 1, half, stride=2), :]
        return split(jnp.concatenate([real, imag], axis=0))

    for at in range(0, u, 2):
        for n, part in enumerate(row_gate(lambda n: column(at + n), w, l)):
            keep(at + n, part[:half].reshape(v, j, k, l), part[half:].reshape(v, j, k, l))
    w = upper_weight(gate_ref[2])
    apply_rows(hi_ref, lo_ref, w, 1, keeper(hi_ref, lo_ref, 1))
    w = middle_weight(gate_ref, 4, spect)
    low = lower_weight(gate_ref[0], gate_ref[3])

    def through_low(one, real, imag):
        x = jnp.concatenate([real.reshape(half, l), imag.reshape(half, l)], axis=1)
        real, imag = lower_rows(*split(x), low)
        keep(one, real.reshape(v, j, k, l), imag.reshape(v, j, k, l))

    apply_rows(hi_ref, lo_ref, w, 0, through_low)
    cosine, sine = rotation(angle_ref, 0, l)
    put_rows(
        w_ref, 0, upper_weight(gate_ref[5], cosine, sine), k, mask_of(name, count, (u, v))
    )
    apply_rows(hi_ref, lo_ref, (w_ref[0, 0], w_ref[0, 1]), 1, sender(outs, order, (u, v)))


def exponentials(high_ref, low_ref, segment, c_ref, s_ref):
    width = c_ref.shape[1]
    for at in range(0, high_ref.shape[1], width):
        row = high_ref[segment : segment + 1, at : at + width]
        c_ref[at : at + width] = jnp.broadcast_to(jnp.cos(row), (width, width)).T
        s_ref[at : at + width] = jnp.broadcast_to(jnp.sin(row), (width, width)).T
    low = [low_ref[segment : segment + 1, at : at + width] for at in (0, width)]
    return [(jnp.cos(row), jnp.sin(row)) for row in low]


def fill_table(e_ref, lead, start, kinds, c_ref, s_ref, lows):
    spect, _, k, l = e_ref.shape[-4:]
    for j in range(spect):
        at = pl.ds(start + j // 2, kinds, stride=spect // 2)
        ch = jnp.concatenate([c_ref[at, :]] * (k // kinds), axis=0)
        sh = jnp.concatenate([s_ref[at, :]] * (k // kinds), axis=0)
        cl, sl = lows[j % 2]
        e_ref[(*lead, j, 0)] = ch * cl - sh * sl
        e_ref[(*lead, j, 1)] = sh * cl + ch * sl


def prepare_kernel(spect, segment, came, goes, gate_hbm, angle_hbm, low_ref, high_ref, *rest):
    last = goes is None
    outs, rest = rest[1 : 3 + last], rest[3 + last :]
    w_ref, e_ref = outs[:2]
    gate_ref, angle_ref, c_ref, s_ref, gate_sem, angle_sem = rest
    width = gate_ref.shape[-1]
    v = width // spect // SLAB
    tops = (spect, v)
    gates = load_gates(gate_hbm, segment, gate_ref, gate_sem)
    angle = pltpu.make_async_copy(angle_hbm, angle_ref, angle_sem)
    for copy in gates + [angle]:
        copy.start()
    axis, count, mask = came
    lows = exponentials(high_ref, low_ref, segment - 1, c_ref, s_ref)
    per = high_ref.shape[1] // count
    start = lax.axis_index(axis) * per
    span = SLAB * spect // 2
    for n in range(e_ref.shape[0]):
        fill_table(e_ref, (n,), start + n * span, min(SLAB, per * 2 // spect), c_ref, s_ref, lows)
    if last:
        lows = exponentials(high_ref, low_ref, segment, c_ref, s_ref)
        for a in range(spect):
            for b in range(v):
                fill_table(outs[2], (a, b), (a * v + b) * span, SLAB, c_ref, s_ref, lows)
    for copy in gates + [angle]:
        copy.wait()
    cosine, sine = rotation(angle_ref, segment, width)
    flip = (mask_of(mask, count, tops) % v) * (width // v)
    put(w_ref, 0, lower_weight(gate_ref[0], gate_ref[3]))
    put(w_ref, 1, middle_weight(gate_ref, 1, spect, flip=flip))
    put(w_ref, 2, upper_weight(gate_ref[2]))
    put(w_ref, 3, middle_weight(gate_ref, 4, spect))
    final = upper_weight(gate_ref[5], cosine, sine)
    if last:
        put(w_ref, 4, final)
    else:
        put_rows(w_ref, 4, final, SLAB, mask_of(goes[2], goes[1], tops))


def later_kernel(came, order, out_order, last, *refs):
    slots, (w_ref, e_ref), rest = refs[: len(order)], refs[len(order) : len(order) + 2], refs[
        len(order) + 2 :
    ]
    if last:
        f_ref, o_hbm, hi_ref, lo_ref, o_ref, o_sem = rest
    else:
        outs, (hi_ref, lo_ref) = rest[:-2], rest[-2:]
    u, v, j, _, k, l = hi_ref.shape
    axis, count, mask = came
    top = mask_of(mask, count, (u, v)) // v
    few = u * v // len(order)
    half = v * j * k
    w = [(w_ref[n, 0], w_ref[n, 1]) for n in range(w_ref.shape[0])]

    def arrived(place):
        ref, n = slots[order.index(place // few)], place % few
        ev = n % e_ref.shape[0]
        c, s = e_ref[ev, :, 0], e_ref[ev, :, 1]
        real, imag = ref[n, :, 0], ref[n, :, 1]
        real, imag = real * c - imag * s, real * s + imag * c
        return jnp.concatenate([real.reshape(j * k, l), imag.reshape(j * k, l)], axis=1)

    def column(a):
        x = jnp.concatenate([arrived(a * v + b) for b in range(v)], axis=0)
        real, imag = lower_rows(*split(x), w[0])
        return split(jnp.concatenate([real, imag], axis=0))

    keep = keeper(hi_ref, lo_ref, 0)
    for at in range(0, u, 2):
        for n, part in enumerate(row_gate(lambda n: column(at + n), w[1], l)):
            keep(
                (at + n) ^ top, part[:half].reshape(v, j, k, l), part[half:].reshape(v, j, k, l)
            )
    apply_rows(hi_ref, lo_ref, w[2], 1, keeper(hi_ref, lo_ref, 1))
    apply_rows(hi_ref, lo_ref, w[3], 0, keeper(hi_ref, lo_ref, 0))
    if not last:
        apply_rows(hi_ref, lo_ref, w[4], 1, sender(outs, out_order, (u, v)))
        return

    stride = 2 * j

    def finish(one, real, imag):
        c, s = f_ref[:, :, one, 0], f_ref[:, :, one, 1]
        both = (real * c - imag * s, real * s + imag * c)
        for ri, value in enumerate(both):
            for a in range(u):
                for b in range(v):
                    start = (a * v + b) * k * stride + one * 2 + ri
                    o_ref[pl.ds(start, k, stride=stride), :] = value[a, b]

    apply_rows(hi_ref, lo_ref, w[4], 1, finish)
    block = v * k * stride
    copies = [
        pltpu.make_async_copy(
            o_ref.at[pl.ds(a * block, block)], o_hbm.at[pl.ds(a * block, block)], o_sem.at[a]
        )
        for a in range(u)
    ]
    for copy in copies:
        copy.start()
    for copy in copies:
        copy.wait()


ORDERS = {4: (1, 2, 3, 0), 8: (6, 4, 7, 5, 2, 3, 1, 0)}


def body(amplitudes, gate_blocks, phase_low, phase_high, phase_global):
    cells = amplitudes.shape[1]
    segments, per_segment, _, width, _ = gate_blocks.shape
    spect = cells // (width * width)
    k = SLAB
    v = width // spect // k
    dims = (spect, v, spect, 2, k, width)
    tops = spect * v
    rows = 2 * cells // width
    highs = phase_high.shape[1]
    vmem = pl.BlockSpec(memory_space=pltpu.VMEM)
    anywhere = pl.BlockSpec(memory_space=pl.ANY)
    hbm = pl.BlockSpec(memory_space=pltpu.HBM)
    state_scratch = [pltpu.VMEM(dims, BF16), pltpu.VMEM(dims, BF16)]
    gate_scratch = [
        pltpu.VMEM(gate_blocks.shape[1:], F32),
        pltpu.VMEM((1, segments), F32),
    ]
    in_hbm = functools.partial(pltpu.with_memory_space_constraint, memory_space=pltpu.HBM)
    gates, angles = in_hbm(gate_blocks), in_hbm(
        phase_global.transpose(1, 2, 0).reshape(1, segments)
    )
    params = pltpu.CompilerParams(vmem_limit_bytes=VMEM_LIMIT)

    def cost(scale):
        return pl.CostEstimate(
            flops=int(40 * cells * width * scale),
            bytes_accessed=int(8 * cells * scale),
            transcendentals=0,
        )

    def plan(segment):
        name = "qb" if segment == 1 else "qa"
        count = lax.axis_size(name)
        if count in ORDERS and count <= tops:
            return name, count, name, ORDERS[count]
        return name, count, None, tuple(range(tops))

    def slots_of(order):
        shape = (tops // len(order),) + dims[2:]
        return [jax.ShapeDtypeStruct(shape, F32) for _ in order]

    def exchange(values, segment):
        name, count, mask, order = plan(segment)
        if mask is not None:
            return [
                lax.ppermute(value, name, [(i, i ^ place) for i in range(count)])
                if place
                else value
                for value, place in zip(values, order)
            ]
        value = jnp.concatenate(values, axis=0)
        more = max(count // tops, 1)
        blocks = value.reshape(tops, spect * 2, more, k // more, width)
        blocks = blocks.transpose(0, 2, 1, 3, 4).reshape(count, rows // count, width)
        moved = lax.all_to_all(blocks, name, split_axis=0, concat_axis=0, tiled=True)
        moved = moved.reshape(tops, more, spect * 2, k // more, width)
        moved = moved.transpose(0, 2, 1, 3, 4).reshape((tops, 1) + dims[2:])
        return [moved[i] for i in range(tops)]

    x = amplitudes.reshape(2, cells // width, width).transpose(1, 0, 2).reshape(rows, width)
    name, count, mask, order = plan(0)
    state = pl.pallas_call(
        functools.partial(first_kernel, spect, mask, count, order),
        out_shape=slots_of(order),
        in_specs=[hbm] * 3,
        out_specs=[vmem] * len(order),
        scratch_shapes=state_scratch
        + [pltpu.VMEM((rows, width), F32)]
        + gate_scratch
        + [
            pltpu.VMEM((1, 2, 2 * width, 2 * width), BF16),
            pltpu.SemaphoreType.DMA((per_segment,)),
            pltpu.SemaphoreType.DMA((spect + 1,)),
        ],
        compiler_params=params,
        cost_estimate=cost(1),
    )(in_hbm(x), gates, angles)

    w_shape = (per_segment - 1, 2, 2 * width, 2 * width)
    for segment in range(1, segments):
        before = state[-1]
        last = segment == segments - 1
        in_axis, in_count, in_mask, in_order = plan(segment - 1)
        came, goes, out_order = (in_axis, in_count, in_mask), None, None
        if not last:
            out_axis, out_count, out_mask, out_order = plan(segment)
            goes = (out_axis, out_count, out_mask)
        e_shape = (max(v * spect // in_count, 1),) + dims[2:]
        tables = [w_shape, e_shape] + ([dims] if last else [])
        made = pl.pallas_call(
            functools.partial(prepare_kernel, spect, segment, came, goes),
            out_shape=[
                jax.ShapeDtypeStruct(shape, F32 if n else BF16) for n, shape in enumerate(tables)
            ],
            in_specs=[hbm, hbm, vmem, vmem, anywhere],
            out_specs=[vmem] * len(tables),
            scratch_shapes=gate_scratch
            + [
                pltpu.VMEM((highs, width), F32),
                pltpu.VMEM((highs, width), F32),
                pltpu.SemaphoreType.DMA((per_segment,)),
                pltpu.SemaphoreType.DMA(()),
            ],
            compiler_params=params,
            cost_estimate=cost(1),
        )(gates, angles, phase_low, phase_high, before)
        state = exchange(state, segment - 1)
        state = pl.pallas_call(
            functools.partial(later_kernel, came, in_order, out_order, last),
            out_shape=jax.ShapeDtypeStruct((rows, width), F32) if last else slots_of(out_order),
            in_specs=[vmem] * (len(in_order) + len(made)),
            out_specs=hbm if last else [vmem] * len(out_order),
            scratch_shapes=state_scratch
            + (
                [pltpu.VMEM((rows, width), F32), pltpu.SemaphoreType.DMA((spect,))]
                if last
                else []
            ),
            compiler_params=params,
            cost_estimate=cost(1),
        )(*state, *made)
    return state.reshape(cells // width, 2, width).transpose(1, 0, 2).reshape(2, cells)


def solution(mesh):
    return jax.shard_map(
        body,
        mesh=mesh,
        in_specs=(P(None, ("qa", "qb")), P(), P(), P(), P(None, "qa", "qb")),
        out_specs=P(None, ("qa", "qb")),
        check_vma=False,
    )
```

```python
import functools

import jax
import jax.numpy as jnp
from jax import lax
from jax.experimental import pallas as pl
from jax.experimental.pallas import tpu as pltpu
from jax.sharding import PartitionSpec as P

F32 = jnp.float32
BF16 = jnp.bfloat16
SLAB = 16
VMEM_LIMIT = 16 << 20


def split(x):
    high = x.astype(BF16)
    return high, (x - high.astype(F32)).astype(BF16)


def dot(a, b):
    return jnp.dot(a, b, preferred_element_type=F32)


def dot3(ah, al, bh, bl):
    return dot(ah, bh) + (dot(al, bh) + dot(ah, bl))


def block_of(real, imag):
    top = jnp.concatenate([real, -imag], axis=1)
    low = jnp.concatenate([imag, real], axis=1)
    return jnp.concatenate([top, low], axis=0)


def inner_order(q, width, spect):
    group = SLAB * spect
    return (q // group) * group + (q % spect) * SLAB + (q % group) // spect


def one_hot(rows, cols, test):
    r = lax.broadcasted_iota(jnp.int32, (rows, cols), 0)
    c = lax.broadcasted_iota(jnp.int32, (rows, cols), 1)
    return jnp.where(test(r, c), 1.0, 0.0).astype(BF16)


def rows_inner(ref, width, spect):
    group = SLAB * spect
    return jnp.concatenate(
        [
            ref[pl.ds(top + j, SLAB, stride=spect), :]
            for top in range(0, width, group)
            for j in range(spect)
        ],
        axis=0,
    )


def middle_weight(gate_ref, g, spect, natural=False, flip=0):
    width = gate_ref.shape[-1]
    real = split(rows_inner(gate_ref.at[g, 0], width, spect))
    imag = split(rows_inner(gate_ref.at[g, 1], width, spect))
    if natural:
        return [block_of(r, i) for r, i in zip(real, imag)]
    right = one_hot(width, width, lambda r, c: (c ^ flip) == inner_order(r, width, spect))
    moved = dot(jnp.concatenate([*real, *imag], axis=0), right).astype(BF16)
    part = [moved[n * width : (n + 1) * width] for n in range(4)]
    return [block_of(part[0], part[2]), block_of(part[1], part[3])]


def upper_weight(gate, cosine=None, sine=None):
    real, imag = gate[0], gate[1]
    if cosine is not None:
        real, imag = real * cosine - imag * sine, real * sine + imag * cosine
    return [block_of(r, i) for r, i in zip(split(real), split(imag))]


def compose(first, second):
    width = first[0].shape[-1]
    lh, ll = split(jnp.concatenate([second[0], second[1]], axis=1))
    top = jnp.concatenate([first[0], first[1]], axis=1)
    low = jnp.concatenate([-first[1], first[0]], axis=1)
    rh, rl = split(jnp.concatenate([top, low], axis=0))
    joined = dot3(lh, ll, rh, rl)
    return joined[:, :width], joined[:, width:]


def as_column(row):
    width = row.shape[1]
    return jnp.broadcast_to(row, (width, width)).T


def lower_weight(before, after, lows):
    out = []
    for c, s in lows:
        c, s = as_column(c), as_column(s)
        turned = before[0] * c - before[1] * s, before[0] * s + before[1] * c
        real, imag = compose(turned, after)
        out.append([block_of(r, -i) for r, i in zip(split(real.T), split(imag.T))])
    return out


def put_rows(w_ref, n, pair, group, mask):
    half = pair[0].shape[0] // 2
    for p, value in enumerate(pair):
        for ri in range(2):
            for g in range(half // group):
                start = pl.multiple_of(ri * half + (g ^ mask) * group, group)
                at = ri * half + g * group
                w_ref[n, p, pl.ds(start, group), :] = value[at : at + group]


def put(w_ref, n, pair):
    w_ref[n, 0] = pair[0]
    w_ref[n, 1] = pair[1]


def rotation(ref, segment, width):
    theta = jnp.broadcast_to(ref[0:1, segment : segment + 1], (1, width))
    return jnp.cos(theta), jnp.sin(theta)


def lower_rows(xh, xl, w):
    y = dot3(xh, xl, w[0], w[1])
    half = y.shape[1] // 2
    return y[:, :half], y[:, half:]


def side_by_side(x):
    *lead, _, k, l = x.shape
    rows = functools.reduce(lambda m, n: m * n, lead, k)
    x = x.reshape(rows // k, 2, k, l)
    return jnp.concatenate([x[:, 0].reshape(rows, l), x[:, 1].reshape(rows, l)], axis=1)


def row_gate(take, w, l):
    first, second = take(0), take(1)
    y = dot3(
        w[0],
        w[1],
        jnp.concatenate([first[0], second[0]], axis=1),
        jnp.concatenate([first[1], second[1]], axis=1),
    )
    return y[:, :l], y[:, l:]


def apply_rows(hi_ref, lo_ref, w, axis, done, pairs=None):
    u, v, j, _, k, l = hi_ref.shape
    count, inner = (u, (v, j)) if axis == 0 else (j, (u, v))
    half = inner[0] * inner[1] * k

    def column(ref, one):
        part = ref[one] if axis == 0 else ref[:, :, one]
        return jnp.concatenate(
            [part[:, :, 0].reshape(half, l), part[:, :, 1].reshape(half, l)], axis=0
        )

    for at in range(0, count, 2) if pairs is None else pairs:
        parts = row_gate(lambda n: (column(hi_ref, at + n), column(lo_ref, at + n)), w, l)
        for n, part in enumerate(parts):
            done(at + n, part[:half].reshape(*inner, k, l), part[half:].reshape(*inner, k, l))


def keeper(hi_ref, lo_ref, axis):
    def keep(one, real, imag):
        for ri, value in ((0, real), (1, imag)):
            high, low = split(value)
            if axis == 0:
                hi_ref[one, :, :, ri] = high
                lo_ref[one, :, :, ri] = low
            else:
                hi_ref[:, :, one, ri] = high
                lo_ref[:, :, one, ri] = low

    return keep


def mask_of(name, count, dims):
    if name is None:
        return 0
    return lax.axis_index(name) * (dims[0] * dims[1] // count)


def sender(outs, order, dims):
    tops = dims[0] * dims[1]
    few = tops // len(outs)

    def put_out(one, real, imag):
        for ri, value in ((0, real), (1, imag)):
            value = value.reshape(len(outs), few, *value.shape[2:])
            for ref, place in zip(outs, order):
                ref[:, one, ri] = value[place]

    return put_out


def load_gates(gate_hbm, segment, gate_ref, sems, wanted):
    return {
        g: pltpu.make_async_copy(gate_hbm.at[segment, g], gate_ref.at[g], sems.at[g])
        for g in wanted
    }


def first_kernel(spect, name, count, order, x_hbm, gate_hbm, angle_hbm, *rest):
    outs = rest[: len(order)]
    hi_ref, lo_ref, x_ref, gate_ref, angle_ref, w_ref, gate_sem, x_sem = rest[len(order) :]
    u, v, j, _, k, l = hi_ref.shape
    gates = load_gates(gate_hbm, 0, gate_ref, gate_sem, (1, 2, 4, 5))
    block = 2 * v * j * k
    parts = [
        pltpu.make_async_copy(
            x_hbm.at[pl.ds(a * block, block)], x_ref.at[pl.ds(a * block, block)], x_sem.at[a]
        )
        for a in range(u)
    ]
    angle = pltpu.make_async_copy(angle_hbm, angle_ref, x_sem.at[u])
    wanted = [gates[1], *parts, gates[2]]
    others = [gates[4], gates[5], angle]
    for copy in wanted + others:
        copy.start()
    for copy in wanted:
        copy.wait()
    half = block // 2
    keep = keeper(hi_ref, lo_ref, 0)
    w = middle_weight(gate_ref, 1, spect, True)

    def column(a):
        real = x_ref[pl.ds(a * block, half, stride=2), :]
        imag = x_ref[pl.ds(a * block + 1, half, stride=2), :]
        return split(jnp.concatenate([real, imag], axis=0))

    for at in range(0, u, 2):
        for n, part in enumerate(row_gate(lambda n: column(at + n), w, l)):
            keep(at + n, part[:half].reshape(v, j, k, l), part[half:].reshape(v, j, k, l))
    w = upper_weight(gate_ref[2])
    apply_rows(hi_ref, lo_ref, w, 1, keeper(hi_ref, lo_ref, 1))
    for copy in others:
        copy.wait()
    w = middle_weight(gate_ref, 4, spect)
    apply_rows(hi_ref, lo_ref, w, 0, keep)
    cosine, sine = rotation(angle_ref, 0, l)
    put_rows(
        w_ref, 0, upper_weight(gate_ref[5], cosine, sine), k, mask_of(name, count, (u, v))
    )
    apply_rows(hi_ref, lo_ref, (w_ref[0, 0], w_ref[0, 1]), 1, sender(outs, order, (u, v)))


def exponentials(high_ref, low_ref, segment, c_ref, s_ref):
    width = c_ref.shape[1]
    for at in range(0, high_ref.shape[1], width):
        row = high_ref[segment : segment + 1, at : at + width]
        c_ref[at : at + width] = as_column(jnp.cos(row))
        s_ref[at : at + width] = as_column(jnp.sin(row))
    low = [low_ref[segment : segment + 1, at : at + width] for at in (0, width)]
    return [(jnp.cos(row), jnp.sin(row)) for row in low]


def fill_table(e_ref, lead, start, kinds, c_ref, s_ref, lows):
    spect, _, k, l = e_ref.shape[-4:]
    for j in range(spect):
        at = pl.ds(start + j // 2, kinds, stride=spect // 2)
        ch = jnp.concatenate([c_ref[at, :]] * (k // kinds), axis=0)
        sh = jnp.concatenate([s_ref[at, :]] * (k // kinds), axis=0)
        if lows is not None:
            cl, sl = lows[j % 2]
            ch, sh = ch * cl - sh * sl, sh * cl + ch * sl
        e_ref[(*lead, j, 0)] = ch
        e_ref[(*lead, j, 1)] = sh


def prepare_kernel(
    spect, segment, came, goes, joins, gate_hbm, angle_hbm, low_ref, high_ref, *rest
):
    last = goes is None
    outs, rest = rest[1 : 3 + last], rest[3 + last :]
    w_ref, e_ref = outs[:2]
    gate_ref, angle_ref, old_ref, c_ref, s_ref, gate_sem, old_sem = rest
    width = gate_ref.shape[-1]
    v = width // spect // SLAB
    tops = (spect, v)
    wanted = (0, 1, 2, 3, 4, 5) if joins else (1, 2, 4, 5)
    copies = list(load_gates(gate_hbm, segment, gate_ref, gate_sem, wanted).values())
    if joins:
        copies += [
            pltpu.make_async_copy(gate_hbm.at[segment - 1, g], old_ref.at[n], old_sem.at[n])
            for n, g in enumerate((0, 3))
        ]
    copies.append(pltpu.make_async_copy(angle_hbm, angle_ref, old_sem.at[2]))
    for copy in copies:
        copy.start()
    axis, count, mask = came
    lows = exponentials(high_ref, low_ref, segment - 1, c_ref, s_ref)
    per = high_ref.shape[1] // count
    start = lax.axis_index(axis) * per
    span = SLAB * spect // 2
    kinds = min(SLAB, per * 2 // spect)
    for n in range(e_ref.shape[0]):
        fill_table(
            e_ref, (n,), start + n * span, kinds, c_ref, s_ref, None if joins else lows
        )
    if last:
        ends = exponentials(high_ref, low_ref, segment, c_ref, s_ref)
        for a in range(spect):
            for b in range(v):
                fill_table(outs[2], (a, b), (a * v + b) * span, SLAB, c_ref, s_ref, ends)
    for copy in copies:
        copy.wait()
    cosine, sine = rotation(angle_ref, segment, width)
    flip = (mask_of(mask, count, tops) % v) * (width // v)
    put(w_ref, 0, middle_weight(gate_ref, 1, spect, flip=flip))
    put(w_ref, 1, upper_weight(gate_ref[2]))
    put(w_ref, 2, middle_weight(gate_ref, 4, spect))
    final = upper_weight(gate_ref[5], cosine, sine)
    if last:
        put(w_ref, 3, final)
    else:
        put_rows(w_ref, 3, final, SLAB, mask_of(goes[2], goes[1], tops))
    if joins:
        before = compose(old_ref[0], old_ref[1])
        after = compose(gate_ref[0], gate_ref[3])
        for n, pair in enumerate(lower_weight(before, after, lows)):
            put(w_ref, 4 + n, pair)


def later_kernel(came, order, out_order, last, *refs):
    slots, (w_ref, e_ref), rest = refs[: len(order)], refs[len(order) : len(order) + 2], refs[
        len(order) + 2 :
    ]
    if last:
        f_ref, o_hbm, hi_ref, lo_ref, o_ref, o_sem = rest
    else:
        outs, (hi_ref, lo_ref) = rest[:-2], rest[-2:]
    u, v, j, _, k, l = hi_ref.shape
    axis, count, mask = came
    top = mask_of(mask, count, (u, v)) // v
    few = u * v // len(order)
    half = v * j * k
    w = [(w_ref[n, 0], w_ref[n, 1]) for n in range(w_ref.shape[0])]

    def arrived(place):
        ref, n = slots[order.index(place // few)], place % few
        ev = n % e_ref.shape[0]
        c, s = e_ref[ev, :, 0], e_ref[ev, :, 1]
        real, imag = ref[n, :, 0], ref[n, :, 1]
        return real * c - imag * s, real * s + imag * c

    def columns(at):
        both = [arrived(place) for place in range(at * v, (at + 2) * v)]
        real, imag = (jnp.stack([one[n] for one in both]) for n in range(2))
        if len(w) > 4:
            lows = []
            for q in range(2):
                flat = [
                    x.reshape(2 * v, j // 2, 2, k, l)[:, :, q].reshape(v * j * k, l)
                    for x in (real, imag)
                ]
                part = lower_rows(*split(jnp.concatenate(flat, axis=1)), w[4 + q])
                lows.append([x.reshape(2 * v, j // 2, k, l) for x in part])
            real, imag = (jnp.stack([lows[0][n], lows[1][n]], axis=2) for n in range(2))
        real, imag = real.reshape(2, half, l), imag.reshape(2, half, l)
        return [split(jnp.concatenate([real[n], imag[n]], axis=0)) for n in range(2)]

    keep = keeper(hi_ref, lo_ref, 0)
    for at in range(0, u, 2):
        pair = columns(at)
        for n, part in enumerate(row_gate(lambda n: pair[n], w[0], l)):
            keep(
                (at + n) ^ top, part[:half].reshape(v, j, k, l), part[half:].reshape(v, j, k, l)
            )
    apply_rows(hi_ref, lo_ref, w[1], 1, keeper(hi_ref, lo_ref, 1))
    apply_rows(hi_ref, lo_ref, w[2], 0, keeper(hi_ref, lo_ref, 0))
    if not last:
        apply_rows(hi_ref, lo_ref, w[3], 1, sender(outs, out_order, (u, v)))
        return

    stride = 2 * j

    def finish(one, real, imag):
        c, s = f_ref[:, :, one, 0], f_ref[:, :, one, 1]
        both = (real * c - imag * s, real * s + imag * c)
        for ri, value in enumerate(both):
            for a in range(u):
                for b in range(v):
                    start = (a * v + b) * k * stride + one * 2 + ri
                    o_ref[pl.ds(start, k, stride=stride), :] = value[a, b]

    apply_rows(hi_ref, lo_ref, w[3], 1, finish)
    block = v * k * stride
    copies = [
        pltpu.make_async_copy(
            o_ref.at[pl.ds(a * block, block)], o_hbm.at[pl.ds(a * block, block)], o_sem.at[a]
        )
        for a in range(u)
    ]
    for copy in copies:
        copy.start()
    for copy in copies:
        copy.wait()


ORDERS = {4: (1, 2, 3, 0), 8: (6, 4, 7, 5, 2, 3, 1, 0)}


def body(amplitudes, gate_blocks, phase_low, phase_high, phase_global):
    cells = amplitudes.shape[1]
    segments, per_segment, _, width, _ = gate_blocks.shape
    spect = cells // (width * width)
    k = SLAB
    v = width // spect // k
    dims = (spect, v, spect, 2, k, width)
    tops = spect * v
    rows = 2 * cells // width
    highs = phase_high.shape[1]
    vmem = pl.BlockSpec(memory_space=pltpu.VMEM)
    anywhere = pl.BlockSpec(memory_space=pl.ANY)
    hbm = pl.BlockSpec(memory_space=pltpu.HBM)
    state_scratch = [pltpu.VMEM(dims, BF16), pltpu.VMEM(dims, BF16)]
    gate_scratch = [
        pltpu.VMEM(gate_blocks.shape[1:], F32),
        pltpu.VMEM((1, segments), F32),
    ]
    in_hbm = functools.partial(pltpu.with_memory_space_constraint, memory_space=pltpu.HBM)
    gates, angles = in_hbm(gate_blocks), in_hbm(
        phase_global.transpose(1, 2, 0).reshape(1, segments)
    )
    params = pltpu.CompilerParams(vmem_limit_bytes=VMEM_LIMIT)

    def cost(scale):
        return pl.CostEstimate(
            flops=int(40 * cells * width * scale),
            bytes_accessed=int(8 * cells * scale),
            transcendentals=0,
        )

    def plan(segment):
        name = "qb" if segment == 1 else "qa"
        count = lax.axis_size(name)
        if count in ORDERS and count <= tops:
            return name, count, name, ORDERS[count]
        return name, count, None, tuple(range(tops))

    def slots_of(order):
        shape = (tops // len(order),) + dims[2:]
        return [jax.ShapeDtypeStruct(shape, F32) for _ in order]

    def exchange(values, segment):
        name, count, mask, order = plan(segment)
        if mask is not None:
            return [
                lax.ppermute(value, name, [(i, i ^ place) for i in range(count)])
                if place
                else value
                for value, place in zip(values, order)
            ]
        value = jnp.concatenate(values, axis=0)
        more = max(count // tops, 1)
        blocks = value.reshape(tops, spect * 2, more, k // more, width)
        blocks = blocks.transpose(0, 2, 1, 3, 4).reshape(count, rows // count, width)
        moved = lax.all_to_all(blocks, name, split_axis=0, concat_axis=0, tiled=True)
        moved = moved.reshape(tops, more, spect * 2, k // more, width)
        moved = moved.transpose(0, 2, 1, 3, 4).reshape((tops, 1) + dims[2:])
        return [moved[i] for i in range(tops)]

    x = amplitudes.reshape(2, cells // width, width).transpose(1, 0, 2).reshape(rows, width)
    name, count, mask, order = plan(0)
    state = pl.pallas_call(
        functools.partial(first_kernel, spect, mask, count, order),
        out_shape=slots_of(order),
        in_specs=[hbm] * 3,
        out_specs=[vmem] * len(order),
        scratch_shapes=state_scratch
        + [pltpu.VMEM((rows, width), F32)]
        + gate_scratch
        + [
            pltpu.VMEM((1, 2, 2 * width, 2 * width), BF16),
            pltpu.SemaphoreType.DMA((per_segment,)),
            pltpu.SemaphoreType.DMA((spect + 1,)),
        ],
        compiler_params=params,
        cost_estimate=cost(1),
    )(in_hbm(x), gates, angles)

    for segment in range(1, segments):
        before = state[-1]
        last = segment == segments - 1
        in_axis, in_count, in_mask, in_order = plan(segment - 1)
        came, goes, out_order = (in_axis, in_count, in_mask), None, None
        if not last:
            out_axis, out_count, out_mask, out_order = plan(segment)
            goes = (out_axis, out_count, out_mask)
        e_shape = (max(v * spect // in_count, 1),) + dims[2:]
        joins = segment % 2 == 1
        w_shape = (6 if joins else 4, 2, 2 * width, 2 * width)
        tables = [w_shape, e_shape] + ([dims] if last else [])
        made = pl.pallas_call(
            functools.partial(prepare_kernel, spect, segment, came, goes, joins),
            out_shape=[
                jax.ShapeDtypeStruct(shape, F32 if n else BF16) for n, shape in enumerate(tables)
            ],
            in_specs=[hbm, hbm, vmem, vmem, anywhere],
            out_specs=[vmem] * len(tables),
            scratch_shapes=gate_scratch
            + [
                pltpu.VMEM((2,) + gate_blocks.shape[2:], F32),
                pltpu.VMEM((highs, width), F32),
                pltpu.VMEM((highs, width), F32),
                pltpu.SemaphoreType.DMA((per_segment,)),
                pltpu.SemaphoreType.DMA((3,)),
            ],
            compiler_params=params,
            cost_estimate=cost(1),
        )(gates, angles, phase_low, phase_high, before)
        state = exchange(state, segment - 1)
        state = pl.pallas_call(
            functools.partial(later_kernel, came, in_order, out_order, last),
            out_shape=jax.ShapeDtypeStruct((rows, width), F32) if last else slots_of(out_order),
            in_specs=[vmem] * (len(in_order) + len(made)),
            out_specs=hbm if last else [vmem] * len(out_order),
            scratch_shapes=state_scratch
            + (
                [pltpu.VMEM((rows, width), F32), pltpu.SemaphoreType.DMA((spect,))]
                if last
                else []
            ),
            compiler_params=params,
            cost_estimate=cost(1),
        )(*state, *made)
    return state.reshape(cells // width, 2, width).transpose(1, 0, 2).reshape(2, cells)


def solution(mesh):
    return jax.shard_map(
        body,
        mesh=mesh,
        in_specs=(P(None, ("qa", "qb")), P(), P(), P(), P(None, "qa", "qb")),
        out_specs=P(None, ("qa", "qb")),
        check_vma=False,
    )
```

```python
import functools

import jax
import jax.numpy as jnp
from jax import lax
from jax.experimental import pallas as pl
from jax.experimental.pallas import tpu as pltpu
from jax.sharding import PartitionSpec as P

F32 = jnp.float32
BF16 = jnp.bfloat16
SLAB = 16
VMEM_LIMIT = 16 << 20


def split(x):
    high = x.astype(BF16)
    return high, (x - high.astype(F32)).astype(BF16)


def dot(a, b):
    return jnp.dot(a, b, preferred_element_type=F32)


def dot3(ah, al, bh, bl):
    return dot(ah, bh) + (dot(al, bh) + dot(ah, bl))


def block_of(real, imag):
    top = jnp.concatenate([real, -imag], axis=1)
    low = jnp.concatenate([imag, real], axis=1)
    return jnp.concatenate([top, low], axis=0)


def inner_order(q, width, spect):
    group = SLAB * spect
    return (q // group) * group + (q % spect) * SLAB + (q % group) // spect


def one_hot(rows, cols, test):
    r = lax.broadcasted_iota(jnp.int32, (rows, cols), 0)
    c = lax.broadcasted_iota(jnp.int32, (rows, cols), 1)
    return jnp.where(test(r, c), 1.0, 0.0).astype(BF16)


def rows_inner(ref, width, spect):
    group = SLAB * spect
    return jnp.concatenate(
        [
            ref[pl.ds(top + j, SLAB, stride=spect), :]
            for top in range(0, width, group)
            for j in range(spect)
        ],
        axis=0,
    )


def middle_weight(gate_ref, g, spect, natural=False, flip=0):
    width = gate_ref.shape[-1]
    real = split(rows_inner(gate_ref.at[g, 0], width, spect))
    imag = split(rows_inner(gate_ref.at[g, 1], width, spect))
    if natural:
        return [block_of(r, i) for r, i in zip(real, imag)]
    right = one_hot(width, width, lambda r, c: (c ^ flip) == inner_order(r, width, spect))
    moved = dot(jnp.concatenate([*real, *imag], axis=0), right).astype(BF16)
    part = [moved[n * width : (n + 1) * width] for n in range(4)]
    return [block_of(part[0], part[2]), block_of(part[1], part[3])]


def upper_weight(gate, cosine=None, sine=None):
    real, imag = gate[0], gate[1]
    if cosine is not None:
        real, imag = real * cosine - imag * sine, real * sine + imag * cosine
    return [block_of(r, i) for r, i in zip(split(real), split(imag))]


def compose(first, second):
    width = first[0].shape[-1]
    lh, ll = split(jnp.concatenate([second[0], second[1]], axis=1))
    top = jnp.concatenate([first[0], first[1]], axis=1)
    low = jnp.concatenate([-first[1], first[0]], axis=1)
    rh, rl = split(jnp.concatenate([top, low], axis=0))
    joined = dot3(lh, ll, rh, rl)
    return joined[:, :width], joined[:, width:]


def as_column(row):
    width = row.shape[1]
    return jnp.broadcast_to(row, (width, width)).T


def lower_weight(before, after, lows):
    out = []
    for c, s in lows:
        c, s = as_column(c), as_column(s)
        turned = before[0] * c - before[1] * s, before[0] * s + before[1] * c
        real, imag = compose(turned, after)
        out.append([block_of(r, -i) for r, i in zip(split(real.T), split(imag.T))])
    return out


def put_rows(w_ref, n, pair, group, mask):
    half = pair[0].shape[0] // 2
    for p, value in enumerate(pair):
        for ri in range(2):
            for g in range(half // group):
                start = pl.multiple_of(ri * half + (g ^ mask) * group, group)
                at = ri * half + g * group
                w_ref[n, p, pl.ds(start, group), :] = value[at : at + group]


def put(w_ref, n, pair):
    w_ref[n, 0] = pair[0]
    w_ref[n, 1] = pair[1]


def rotation(ref, segment, width):
    theta = jnp.broadcast_to(ref[0:1, segment : segment + 1], (1, width))
    return jnp.cos(theta), jnp.sin(theta)


def lower_rows(xh, xl, w):
    y = dot3(xh, xl, w[0], w[1])
    half = y.shape[1] // 2
    return y[:, :half], y[:, half:]


def side_by_side(x):
    *lead, _, k, l = x.shape
    rows = functools.reduce(lambda m, n: m * n, lead, k)
    x = x.reshape(rows // k, 2, k, l)
    return jnp.concatenate([x[:, 0].reshape(rows, l), x[:, 1].reshape(rows, l)], axis=1)


def row_gate(take, w, l):
    first, second = take(0), take(1)
    y = dot3(
        w[0],
        w[1],
        jnp.concatenate([first[0], second[0]], axis=1),
        jnp.concatenate([first[1], second[1]], axis=1),
    )
    return y[:, :l], y[:, l:]


def apply_rows(hi_ref, lo_ref, w, axis, done, pairs=None):
    u, v, j, _, k, l = hi_ref.shape
    count, inner = (u, (v, j)) if axis == 0 else (j, (u, v))
    half = inner[0] * inner[1] * k

    def column(ref, one):
        part = ref[one] if axis == 0 else ref[:, :, one]
        return jnp.concatenate(
            [part[:, :, 0].reshape(half, l), part[:, :, 1].reshape(half, l)], axis=0
        )

    for at in range(0, count, 2) if pairs is None else pairs:
        parts = row_gate(lambda n: (column(hi_ref, at + n), column(lo_ref, at + n)), w, l)
        for n, part in enumerate(parts):
            done(at + n, part[:half].reshape(*inner, k, l), part[half:].reshape(*inner, k, l))


def keeper(hi_ref, lo_ref, axis):
    def keep(one, real, imag):
        for ri, value in ((0, real), (1, imag)):
            high, low = split(value)
            if axis == 0:
                hi_ref[one, :, :, ri] = high
                lo_ref[one, :, :, ri] = low
            else:
                hi_ref[:, :, one, ri] = high
                lo_ref[:, :, one, ri] = low

    return keep


def mask_of(name, count, dims):
    if name is None:
        return 0
    return lax.axis_index(name) * (dims[0] * dims[1] // count)


def sender(outs, order, dims):
    tops = dims[0] * dims[1]
    few = tops // len(outs)

    def put_out(one, real, imag):
        for ri, value in ((0, real), (1, imag)):
            value = value.reshape(len(outs), few, *value.shape[2:])
            for ref, place in zip(outs, order):
                ref[:, one, ri] = value[place]

    return put_out


def load_gates(gate_hbm, segment, gate_ref, sems, wanted):
    return {
        g: pltpu.make_async_copy(gate_hbm.at[segment, g], gate_ref.at[g], sems.at[g])
        for g in wanted
    }


def first_kernel(spect, name, count, order, x_hbm, gate_hbm, angle_hbm, *rest):
    outs = rest[: len(order)]
    hi_ref, lo_ref, x_ref, gate_ref, angle_ref, w_ref, gate_sem, x_sem = rest[len(order) :]
    u, v, j, _, k, l = hi_ref.shape
    gates = load_gates(gate_hbm, 0, gate_ref, gate_sem, (1, 2, 4, 5))
    block = 2 * v * j * k
    parts = [
        pltpu.make_async_copy(
            x_hbm.at[pl.ds(a * block, block)], x_ref.at[pl.ds(a * block, block)], x_sem.at[a]
        )
        for a in range(u)
    ]
    angle = pltpu.make_async_copy(angle_hbm, angle_ref, x_sem.at[u])
    for copy in [gates[1], *parts, gates[2], gates[4], gates[5], angle]:
        copy.start()
    half = block // 2
    keep = keeper(hi_ref, lo_ref, 0)
    for copy in [gates[1], gates[2], gates[4], gates[5], angle, *parts]:
        copy.wait()
    w = middle_weight(gate_ref, 1, spect, True)

    def column(a):
        real = x_ref[pl.ds(a * block, half, stride=2), :]
        imag = x_ref[pl.ds(a * block + 1, half, stride=2), :]
        return split(jnp.concatenate([real, imag], axis=0))

    for at in range(0, u, 2):
        for n, part in enumerate(row_gate(lambda n: column(at + n), w, l)):
            keep(at + n, part[:half].reshape(v, j, k, l), part[half:].reshape(v, j, k, l))
    w = upper_weight(gate_ref[2])
    apply_rows(hi_ref, lo_ref, w, 1, keeper(hi_ref, lo_ref, 1))
    w = middle_weight(gate_ref, 4, spect)
    apply_rows(hi_ref, lo_ref, w, 0, keep)
    cosine, sine = rotation(angle_ref, 0, l)
    put_rows(
        w_ref, 0, upper_weight(gate_ref[5], cosine, sine), k, mask_of(name, count, (u, v))
    )
    apply_rows(hi_ref, lo_ref, (w_ref[0, 0], w_ref[0, 1]), 1, sender(outs, order, (u, v)))


def exponentials(high_ref, low_ref, segment, c_ref, s_ref):
    width = c_ref.shape[1]
    for at in range(0, high_ref.shape[1], width):
        row = high_ref[segment : segment + 1, at : at + width]
        c_ref[at : at + width] = as_column(jnp.cos(row))
        s_ref[at : at + width] = as_column(jnp.sin(row))
    low = [low_ref[segment : segment + 1, at : at + width] for at in (0, width)]
    return [(jnp.cos(row), jnp.sin(row)) for row in low]


def fill_table(e_ref, lead, start, kinds, c_ref, s_ref, lows):
    spect, _, k, l = e_ref.shape[-4:]
    for j in range(spect):
        at = pl.ds(start + j // 2, kinds, stride=spect // 2)
        ch = jnp.concatenate([c_ref[at, :]] * (k // kinds), axis=0)
        sh = jnp.concatenate([s_ref[at, :]] * (k // kinds), axis=0)
        if lows is not None:
            cl, sl = lows[j % 2]
            ch, sh = ch * cl - sh * sl, sh * cl + ch * sl
        e_ref[(*lead, j, 0)] = ch
        e_ref[(*lead, j, 1)] = sh


def prepare_kernel(
    spect, segment, came, goes, joins, gate_hbm, angle_hbm, low_ref, high_ref, *rest
):
    last = goes is None
    outs, rest = rest[1 : 3 + last], rest[3 + last :]
    w_ref, e_ref = outs[:2]
    gate_ref, angle_ref, old_ref, c_ref, s_ref, gate_sem, old_sem = rest
    width = gate_ref.shape[-1]
    v = width // spect // SLAB
    tops = (spect, v)
    wanted = (0, 1, 2, 3, 4, 5) if joins else (1, 2, 4, 5)
    copies = list(load_gates(gate_hbm, segment, gate_ref, gate_sem, wanted).values())
    if joins:
        copies += [
            pltpu.make_async_copy(gate_hbm.at[segment - 1, g], old_ref.at[n], old_sem.at[n])
            for n, g in enumerate((0, 3))
        ]
    copies.append(pltpu.make_async_copy(angle_hbm, angle_ref, old_sem.at[2]))
    for copy in copies:
        copy.start()
    axis, count, mask = came
    lows = exponentials(high_ref, low_ref, segment - 1, c_ref, s_ref)
    per = high_ref.shape[1] // count
    start = lax.axis_index(axis) * per
    span = SLAB * spect // 2
    kinds = min(SLAB, per * 2 // spect)
    for n in range(e_ref.shape[0]):
        fill_table(
            e_ref, (n,), start + n * span, kinds, c_ref, s_ref, None if joins else lows
        )
    if last:
        ends = exponentials(high_ref, low_ref, segment, c_ref, s_ref)
        for a in range(spect):
            for b in range(v):
                fill_table(outs[2], (a, b), (a * v + b) * span, SLAB, c_ref, s_ref, ends)
    for copy in copies:
        copy.wait()
    cosine, sine = rotation(angle_ref, segment, width)
    flip = (mask_of(mask, count, tops) % v) * (width // v)
    put(w_ref, 0, middle_weight(gate_ref, 1, spect, flip=flip))
    put(w_ref, 1, upper_weight(gate_ref[2]))
    put(w_ref, 2, middle_weight(gate_ref, 4, spect))
    final = upper_weight(gate_ref[5], cosine, sine)
    if last:
        put(w_ref, 3, final)
    else:
        put_rows(w_ref, 3, final, SLAB, mask_of(goes[2], goes[1], tops))
    if joins:
        before = compose(old_ref[0], old_ref[1])
        after = compose(gate_ref[0], gate_ref[3])
        for n, pair in enumerate(lower_weight(before, after, lows)):
            put(w_ref, 4 + n, pair)


def later_kernel(came, order, out_order, last, *refs):
    slots, (w_ref, e_ref), rest = refs[: len(order)], refs[len(order) : len(order) + 2], refs[
        len(order) + 2 :
    ]
    if last:
        f_ref, o_hbm, hi_ref, lo_ref, o_ref, o_sem = rest
    else:
        outs, (hi_ref, lo_ref) = rest[:-2], rest[-2:]
    u, v, j, _, k, l = hi_ref.shape
    axis, count, mask = came
    top = mask_of(mask, count, (u, v)) // v
    few = u * v // len(order)
    half = v * j * k
    w = [(w_ref[n, 0], w_ref[n, 1]) for n in range(w_ref.shape[0])]

    def arrived(place):
        ref, n = slots[order.index(place // few)], place % few
        ev = n % e_ref.shape[0]
        c, s = e_ref[ev, :, 0], e_ref[ev, :, 1]
        real, imag = ref[n, :, 0], ref[n, :, 1]
        return real * c - imag * s, real * s + imag * c

    both = [arrived(place) for place in range(u * v)]
    state = [jnp.stack([one[n] for one in both]) for n in range(2)]
    if len(w) > 4:
        lows = []
        for q in range(2):
            flat = [
                x.reshape(u * v, j // 2, 2, k, l)[:, :, q].reshape(u * half // 2, l)
                for x in state
            ]
            part = lower_rows(*split(jnp.concatenate(flat, axis=1)), w[4 + q])
            lows.append([x.reshape(u * v, j // 2, k, l) for x in part])
        state = [jnp.stack([lows[0][n], lows[1][n]], axis=2) for n in range(2)]
    real, imag = (x.reshape(u, half, l) for x in state)

    def column(a):
        return split(jnp.concatenate([real[a], imag[a]], axis=0))

    keep = keeper(hi_ref, lo_ref, 0)
    for at in range(0, u, 2):
        for n, part in enumerate(row_gate(lambda n: column(at + n), w[0], l)):
            keep(
                (at + n) ^ top, part[:half].reshape(v, j, k, l), part[half:].reshape(v, j, k, l)
            )
    apply_rows(hi_ref, lo_ref, w[1], 1, keeper(hi_ref, lo_ref, 1))
    apply_rows(hi_ref, lo_ref, w[2], 0, keeper(hi_ref, lo_ref, 0))
    if not last:
        apply_rows(hi_ref, lo_ref, w[3], 1, sender(outs, out_order, (u, v)))
        return

    def copies(one):
        return [
            pltpu.make_async_copy(o_ref.at[one, ri], o_hbm.at[:, one, ri], o_sem.at[one, ri])
            for ri in range(2)
        ]

    def finish(one, real, imag):
        c, s = f_ref[:, :, one, 0], f_ref[:, :, one, 1]
        both = (real * c - imag * s, real * s + imag * c)
        for ri, value in enumerate(both):
            o_ref[one, ri] = value.reshape(u * v * k, l)
        for copy in copies(one):
            copy.start()

    apply_rows(hi_ref, lo_ref, w[3], 1, finish)
    for one in range(j):
        for copy in copies(one):
            copy.wait()


ORDERS = {4: (1, 2, 3, 0), 8: (6, 4, 7, 5, 2, 3, 1, 0)}


def body(amplitudes, gate_blocks, phase_low, phase_high, phase_global):
    cells = amplitudes.shape[1]
    segments, per_segment, _, width, _ = gate_blocks.shape
    spect = cells // (width * width)
    k = SLAB
    v = width // spect // k
    dims = (spect, v, spect, 2, k, width)
    tops = spect * v
    rows = 2 * cells // width
    highs = phase_high.shape[1]
    vmem = pl.BlockSpec(memory_space=pltpu.VMEM)
    anywhere = pl.BlockSpec(memory_space=pl.ANY)
    hbm = pl.BlockSpec(memory_space=pltpu.HBM)
    state_scratch = [pltpu.VMEM(dims, BF16), pltpu.VMEM(dims, BF16)]
    gate_scratch = [
        pltpu.VMEM(gate_blocks.shape[1:], F32),
        pltpu.VMEM((1, segments), F32),
    ]
    in_hbm = functools.partial(pltpu.with_memory_space_constraint, memory_space=pltpu.HBM)
    gates, angles = in_hbm(gate_blocks), in_hbm(
        phase_global.transpose(1, 2, 0).reshape(1, segments)
    )
    params = pltpu.CompilerParams(vmem_limit_bytes=VMEM_LIMIT)

    def cost(scale):
        return pl.CostEstimate(
            flops=int(40 * cells * width * scale),
            bytes_accessed=int(8 * cells * scale),
            transcendentals=0,
        )

    def plan(segment):
        name = "qb" if segment == 1 else "qa"
        count = lax.axis_size(name)
        if count in ORDERS and count <= tops:
            return name, count, name, ORDERS[count]
        return name, count, None, tuple(range(tops))

    def slots_of(order):
        shape = (tops // len(order),) + dims[2:]
        return [jax.ShapeDtypeStruct(shape, F32) for _ in order]

    def exchange(values, segment):
        name, count, mask, order = plan(segment)
        if mask is not None:
            return [
                lax.ppermute(value, name, [(i, i ^ place) for i in range(count)])
                if place
                else value
                for value, place in zip(values, order)
            ]
        value = jnp.concatenate(values, axis=0)
        more = max(count // tops, 1)
        blocks = value.reshape(tops, spect * 2, more, k // more, width)
        blocks = blocks.transpose(0, 2, 1, 3, 4).reshape(count, rows // count, width)
        moved = lax.all_to_all(blocks, name, split_axis=0, concat_axis=0, tiled=True)
        moved = moved.reshape(tops, more, spect * 2, k // more, width)
        moved = moved.transpose(0, 2, 1, 3, 4).reshape((tops, 1) + dims[2:])
        return [moved[i] for i in range(tops)]

    x = amplitudes.reshape(2, cells // width, width).transpose(1, 0, 2).reshape(rows, width)
    name, count, mask, order = plan(0)
    state = pl.pallas_call(
        functools.partial(first_kernel, spect, mask, count, order),
        out_shape=slots_of(order),
        in_specs=[hbm] * 3,
        out_specs=[vmem] * len(order),
        scratch_shapes=state_scratch
        + [pltpu.VMEM((rows, width), F32)]
        + gate_scratch
        + [
            pltpu.VMEM((1, 2, 2 * width, 2 * width), BF16),
            pltpu.SemaphoreType.DMA((per_segment,)),
            pltpu.SemaphoreType.DMA((spect + 1,)),
        ],
        compiler_params=params,
        cost_estimate=cost(1),
    )(in_hbm(x), gates, angles)

    out_dims = (tops * k, spect, 2, width)
    for segment in range(1, segments):
        before = state[-1]
        last = segment == segments - 1
        in_axis, in_count, in_mask, in_order = plan(segment - 1)
        came, goes, out_order = (in_axis, in_count, in_mask), None, None
        if not last:
            out_axis, out_count, out_mask, out_order = plan(segment)
            goes = (out_axis, out_count, out_mask)
        e_shape = (max(v * spect // in_count, 1),) + dims[2:]
        joins = segment % 2 == 1
        w_shape = (6 if joins else 4, 2, 2 * width, 2 * width)
        tables = [w_shape, e_shape] + ([dims] if last else [])
        made = pl.pallas_call(
            functools.partial(prepare_kernel, spect, segment, came, goes, joins),
            out_shape=[
                jax.ShapeDtypeStruct(shape, F32 if n else BF16) for n, shape in enumerate(tables)
            ],
            in_specs=[hbm, hbm, vmem, vmem, anywhere],
            out_specs=[vmem] * len(tables),
            scratch_shapes=gate_scratch
            + [
                pltpu.VMEM((2,) + gate_blocks.shape[2:], F32),
                pltpu.VMEM((highs, width), F32),
                pltpu.VMEM((highs, width), F32),
                pltpu.SemaphoreType.DMA((per_segment,)),
                pltpu.SemaphoreType.DMA((3,)),
            ],
            compiler_params=params,
            cost_estimate=cost(1),
        )(gates, angles, phase_low, phase_high, before)
        state = exchange(state, segment - 1)
        state = pl.pallas_call(
            functools.partial(later_kernel, came, in_order, out_order, last),
            out_shape=jax.ShapeDtypeStruct(out_dims, F32) if last else slots_of(out_order),
            in_specs=[vmem] * (len(in_order) + len(made)),
            out_specs=hbm if last else [vmem] * len(out_order),
            scratch_shapes=state_scratch
            + (
                [
                    pltpu.VMEM(out_dims[1:3] + (out_dims[0], width), F32),
                    pltpu.SemaphoreType.DMA(out_dims[1:3]),
                ]
                if last
                else []
            ),
            compiler_params=params,
            cost_estimate=cost(1),
        )(*state, *made)
    return state.reshape(cells // width, 2, width).transpose(1, 0, 2).reshape(2, cells)


def solution(mesh):
    return jax.shard_map(
        body,
        mesh=mesh,
        in_specs=(P(None, ("qa", "qb")), P(), P(), P(), P(None, "qa", "qb")),
        out_specs=P(None, ("qa", "qb")),
        check_vma=False,
    )
```

```python
import functools

import jax
import jax.numpy as jnp
from jax import lax
from jax.experimental import pallas as pl
from jax.experimental.pallas import tpu as pltpu
from jax.sharding import PartitionSpec as P

F32 = jnp.float32
BF16 = jnp.bfloat16
SLAB = 16
VMEM_LIMIT = 16 << 20


def split(x):
    high = x.astype(BF16)
    return high, (x - high.astype(F32)).astype(BF16)


def dot(a, b):
    return jnp.dot(a, b, preferred_element_type=F32)


def dot3(ah, al, bh, bl):
    return dot(ah, bh) + (dot(al, bh) + dot(ah, bl))


def block_of(real, imag):
    top = jnp.concatenate([real, -imag], axis=1)
    low = jnp.concatenate([imag, real], axis=1)
    return jnp.concatenate([top, low], axis=0)


def gate_block(real, imag):
    rows, width = real.shape
    full = block_of(real, imag).reshape(2, rows // SLAB, SLAB, 2 * width)
    return jnp.stack([full[0], full[1]], axis=1).reshape(2 * rows, 2 * width)


def inner_order(q, width, spect):
    group = SLAB * spect
    return (q // group) * group + (q % spect) * SLAB + (q % group) // spect


def one_hot(rows, cols, test):
    r = lax.broadcasted_iota(jnp.int32, (rows, cols), 0)
    c = lax.broadcasted_iota(jnp.int32, (rows, cols), 1)
    return jnp.where(test(r, c), 1.0, 0.0).astype(BF16)


def rows_inner(ref, width, spect):
    group = SLAB * spect
    return jnp.concatenate(
        [
            ref[pl.ds(top + j, SLAB, stride=spect), :]
            for j in range(spect)
            for top in range(0, width, group)
        ],
        axis=0,
    )


def move_columns(real, imag, test):
    width = real[0].shape[1]
    right = one_hot(width, width, test)
    moved = dot(jnp.concatenate([*real, *imag], axis=0), right).astype(BF16)
    part = [moved[n * width : (n + 1) * width] for n in range(4)]
    return part[:2], part[2:]


def middle_weight(gate_ref, g, spect, natural=False, flip=0):
    width = gate_ref.shape[-1]
    real = split(rows_inner(gate_ref.at[g, 0], width, spect))
    imag = split(rows_inner(gate_ref.at[g, 1], width, spect))
    if not natural:
        real, imag = move_columns(
            real, imag, lambda r, c: (c ^ flip) == inner_order(r, width, spect)
        )
    return [gate_block(r, i) for r, i in zip(real, imag)]


def upper_weight(gate, cosine=None, sine=None, flip=None):
    real, imag = gate[0], gate[1]
    if cosine is not None:
        real, imag = real * cosine - imag * sine, real * sine + imag * cosine
    real, imag = split(real), split(imag)
    if flip is not None:
        real, imag = move_columns(real, imag, lambda r, c: (c ^ flip) == r)
    return [gate_block(r, i) for r, i in zip(real, imag)]


def compose(first, second):
    width = first[0].shape[-1]
    lh, ll = split(jnp.concatenate([second[0], second[1]], axis=1))
    top = jnp.concatenate([first[0], first[1]], axis=1)
    low = jnp.concatenate([-first[1], first[0]], axis=1)
    rh, rl = split(jnp.concatenate([top, low], axis=0))
    joined = dot3(lh, ll, rh, rl)
    return joined[:, :width], joined[:, width:]


def as_column(row):
    width = row.shape[1]
    return jnp.broadcast_to(row, (width, width)).T


def lower_weight(before, after, lows):
    out = []
    for c, s in lows:
        c, s = as_column(c), as_column(s)
        turned = before[0] * c - before[1] * s, before[0] * s + before[1] * c
        real, imag = compose(turned, after)
        out.append([block_of(r, -i) for r, i in zip(split(real.T), split(imag.T))])
    return out


def put_rows(w_ref, n, pair, group, mask):
    for p, value in enumerate(pair):
        for g in range(value.shape[0] // group):
            start = pl.multiple_of((g ^ mask) * group, group)
            w_ref[n, p, pl.ds(start, group), :] = value[g * group : (g + 1) * group]


def put(w_ref, n, pair):
    w_ref[n, 0] = pair[0]
    w_ref[n, 1] = pair[1]


def rotation(ref, segment, width):
    theta = jnp.broadcast_to(ref[0:1, segment : segment + 1], (1, width))
    return jnp.cos(theta), jnp.sin(theta)


def lower_rows(xh, xl, w):
    y = dot3(xh, xl, w[0], w[1])
    half = y.shape[1] // 2
    return y[:, :half], y[:, half:]


def side_by_side(x):
    *lead, _, k, l = x.shape
    rows = functools.reduce(lambda m, n: m * n, lead, k)
    x = x.reshape(rows // k, 2, k, l)
    return jnp.concatenate([x[:, 0].reshape(rows, l), x[:, 1].reshape(rows, l)], axis=1)


def row_gate(take, w, l):
    first, second = take(0), take(1)
    y = dot3(
        w[0],
        w[1],
        jnp.concatenate([first[0], second[0]], axis=1),
        jnp.concatenate([first[1], second[1]], axis=1),
    )
    return y[:, :l], y[:, l:]


def finish_rows(parts, lead, k, done):
    for a in range(lead[0]):
        for b in range(lead[1]):
            at = (a * lead[1] + b) * 2 * k
            for n, part in enumerate(parts):
                done(n, (a, b), part[at : at + k], part[at + k : at + 2 * k])


def apply_rows(hi_ref, lo_ref, w, axis, done):
    u, v, j, _, k, l = hi_ref.shape
    count, half = (u, v * j * k) if axis == 0 else (j, u * v * k)

    def column(ref, one):
        part = ref[one] if axis == 0 else ref[:, :, one]
        return jnp.concatenate(
            [part[:, :, 0].reshape(half, l), part[:, :, 1].reshape(half, l)], axis=0
        )

    parts = []
    for at in range(0, count, 2):
        parts += row_gate(lambda n: (column(hi_ref, at + n), column(lo_ref, at + n)), w, l)
    finish_rows(parts, (j, v) if axis == 0 else (u, v), k, done)


def keeper(hi_ref, lo_ref, axis):
    def keep(one, lead, real, imag):
        at = (one, lead[1], lead[0]) if axis == 0 else (*lead, one)
        for ri, value in ((0, real), (1, imag)):
            high, low = split(value)
            hi_ref[(*at, ri)] = high
            lo_ref[(*at, ri)] = low

    return keep


def mask_of(name, count, dims):
    if name is None:
        return 0
    return lax.axis_index(name) * (dims[0] * dims[1] // count)


def sender(outs, order, dims):
    tops = dims[0] * dims[1]
    few = tops // len(outs)

    def put_out(one, lead, real, imag):
        place = lead[0] * dims[1] + lead[1]
        ref = outs[order.index(place // few)]
        ref[place % few, one, 0] = real
        ref[place % few, one, 1] = imag

    return put_out


def load_gates(gate_hbm, segment, gate_ref, sems, wanted):
    return {
        g: pltpu.make_async_copy(gate_hbm.at[segment, g], gate_ref.at[g], sems.at[g])
        for g in wanted
    }


def first_kernel(spect, name, count, order, x_hbm, gate_hbm, angle_hbm, *rest):
    outs = rest[: len(order)]
    hi_ref, lo_ref, x_ref, gate_ref, angle_ref, w_ref, gate_sem, x_sem = rest[len(order) :]
    u, v, j, _, k, l = hi_ref.shape
    gates = load_gates(gate_hbm, 0, gate_ref, gate_sem, (1, 2, 4, 5))
    block = 2 * v * j * k
    pieces = [
        pltpu.make_async_copy(
            x_hbm.at[pl.ds(a * block, block)], x_ref.at[pl.ds(a * block, block)], x_sem.at[a]
        )
        for a in range(u)
    ]
    angle = pltpu.make_async_copy(angle_hbm, angle_ref, x_sem.at[u])
    for copy in [gates[1], *pieces, gates[2], gates[4], gates[5], angle]:
        copy.start()
    half = block // 2
    keep = keeper(hi_ref, lo_ref, 0)
    for copy in [gates[1], gates[2], gates[4], gates[5], angle, *pieces]:
        copy.wait()
    w = middle_weight(gate_ref, 1, spect, True)

    def column(a):
        real = x_ref[pl.ds(a * block, half, stride=2), :]
        imag = x_ref[pl.ds(a * block + 1, half, stride=2), :]
        return split(jnp.concatenate([real, imag], axis=0))

    parts = []
    for at in range(0, u, 2):
        parts += row_gate(lambda n: column(at + n), w, l)
    finish_rows(parts, (j, v), k, keep)
    w = upper_weight(gate_ref[2])
    apply_rows(hi_ref, lo_ref, w, 1, keeper(hi_ref, lo_ref, 1))
    w = middle_weight(gate_ref, 4, spect)
    apply_rows(hi_ref, lo_ref, w, 0, keep)
    cosine, sine = rotation(angle_ref, 0, l)
    put_rows(
        w_ref, 0, upper_weight(gate_ref[5], cosine, sine), 2 * k, mask_of(name, count, (u, v))
    )
    apply_rows(hi_ref, lo_ref, (w_ref[0, 0], w_ref[0, 1]), 1, sender(outs, order, (u, v)))


def exponentials(high_ref, low_ref, segment, c_ref, s_ref):
    width = c_ref.shape[1]
    for at in range(0, high_ref.shape[1], width):
        row = high_ref[segment : segment + 1, at : at + width]
        c_ref[at : at + width] = as_column(jnp.cos(row))
        s_ref[at : at + width] = as_column(jnp.sin(row))
    low = [low_ref[segment : segment + 1, at : at + width] for at in (0, width)]
    return [(jnp.cos(row), jnp.sin(row)) for row in low]


def fill_table(e_ref, lead, start, kinds, c_ref, s_ref, lows):
    spect, _, k, l = e_ref.shape[-4:]
    for j in range(spect):
        at = pl.ds(start + j // 2, kinds, stride=spect // 2)
        ch = jnp.concatenate([c_ref[at, :]] * (k // kinds), axis=0)
        sh = jnp.concatenate([s_ref[at, :]] * (k // kinds), axis=0)
        if lows is not None:
            cl, sl = lows[j % 2]
            ch, sh = ch * cl - sh * sl, sh * cl + ch * sl
        e_ref[(*lead, j, 0)] = ch
        e_ref[(*lead, j, 1)] = sh


def prepare_kernel(
    spect, segment, came, goes, joins, gate_hbm, angle_hbm, low_ref, high_ref, *rest
):
    last = goes is None
    outs, rest = rest[1 : 3 + last], rest[3 + last :]
    w_ref, e_ref = outs[:2]
    gate_ref, angle_ref, old_ref, c_ref, s_ref, gate_sem, old_sem = rest
    width = gate_ref.shape[-1]
    v = width // spect // SLAB
    tops = (spect, v)
    wanted = (0, 1, 2, 3, 4, 5) if joins else (1, 2, 4, 5)
    copies = list(load_gates(gate_hbm, segment, gate_ref, gate_sem, wanted).values())
    if joins:
        copies += [
            pltpu.make_async_copy(gate_hbm.at[segment - 1, g], old_ref.at[n], old_sem.at[n])
            for n, g in enumerate((0, 3))
        ]
    copies.append(pltpu.make_async_copy(angle_hbm, angle_ref, old_sem.at[2]))
    for copy in copies:
        copy.start()
    axis, count, mask = came
    lows = exponentials(high_ref, low_ref, segment - 1, c_ref, s_ref)
    per = high_ref.shape[1] // count
    start = lax.axis_index(axis) * per
    span = SLAB * spect // 2
    kinds = min(SLAB, per * 2 // spect)
    for n in range(e_ref.shape[0]):
        fill_table(
            e_ref, (n,), start + n * span, kinds, c_ref, s_ref, None if joins else lows
        )
    if last:
        ends = exponentials(high_ref, low_ref, segment, c_ref, s_ref)
        for a in range(spect):
            for b in range(v):
                fill_table(outs[2], (a, b), (a * v + b) * span, SLAB, c_ref, s_ref, ends)
    for copy in copies:
        copy.wait()
    cosine, sine = rotation(angle_ref, segment, width)
    arrives = mask_of(mask, count, tops)
    flip, flip_top = (arrives % v) * (width // v), (arrives // v) * (width // spect)
    put(w_ref, 0, middle_weight(gate_ref, 1, spect, flip=flip))
    put(w_ref, 1, upper_weight(gate_ref[2], flip=flip_top))
    put(w_ref, 2, middle_weight(gate_ref, 4, spect))
    final = upper_weight(gate_ref[5], cosine, sine)
    if last:
        put(w_ref, 3, final)
    else:
        put_rows(w_ref, 3, final, 2 * SLAB, mask_of(goes[2], goes[1], tops))
    if joins:
        before = compose(old_ref[0], old_ref[1])
        after = compose(gate_ref[0], gate_ref[3])
        for n, pair in enumerate(lower_weight(before, after, lows)):
            put(w_ref, 4 + n, pair)


def later_kernel(order, out_order, last, *refs):
    slots, (w_ref, e_ref), rest = refs[: len(order)], refs[len(order) : len(order) + 2], refs[
        len(order) + 2 :
    ]
    if last:
        f_ref, o_hbm, hi_ref, lo_ref, o_ref, o_sem = rest
    else:
        outs, (hi_ref, lo_ref) = rest[:-2], rest[-2:]
    u, v, j, _, k, l = hi_ref.shape
    few = u * v // len(order)
    half = v * j * k
    w = [(w_ref[n, 0], w_ref[n, 1]) for n in range(w_ref.shape[0])]

    def arrived(place):
        ref, n = slots[order.index(place // few)], place % few
        ev = n % e_ref.shape[0]
        c, s = e_ref[ev, :, 0], e_ref[ev, :, 1]
        real, imag = ref[n, :, 0], ref[n, :, 1]
        return real * c - imag * s, real * s + imag * c

    both = [arrived(place) for place in range(u * v)]
    state = [jnp.stack([one[n] for one in both]) for n in range(2)]
    if len(w) > 4:
        lows = []
        for q in range(2):
            flat = [
                x.reshape(u * v, j // 2, 2, k, l)[:, :, q].reshape(u * half // 2, l)
                for x in state
            ]
            part = lower_rows(*split(jnp.concatenate(flat, axis=1)), w[4 + q])
            lows.append([x.reshape(u * v, j // 2, k, l) for x in part])
        state = [jnp.stack([lows[0][n], lows[1][n]], axis=2) for n in range(2)]
    real, imag = (x.reshape(u, half, l) for x in state)

    def column(a):
        return split(jnp.concatenate([real[a], imag[a]], axis=0))

    keep = keeper(hi_ref, lo_ref, 0)
    parts = []
    for at in range(0, u, 2):
        parts += row_gate(lambda n: column(at + n), w[0], l)
    finish_rows(parts, (j, v), k, keep)
    apply_rows(hi_ref, lo_ref, w[1], 1, keeper(hi_ref, lo_ref, 1))
    apply_rows(hi_ref, lo_ref, w[2], 0, keeper(hi_ref, lo_ref, 0))
    if not last:
        apply_rows(hi_ref, lo_ref, w[3], 1, sender(outs, out_order, (u, v)))
        return

    def copies(one):
        return [
            pltpu.make_async_copy(o_ref.at[one, ri], o_hbm.at[:, one, ri], o_sem.at[one, ri])
            for ri in range(2)
        ]

    def finish(one, lead, real, imag):
        c, s = (f_ref[(*lead, one, ri)] for ri in range(2))
        at = (lead[0] * v + lead[1]) * k
        o_ref[one, 0, at : at + k] = real * c - imag * s
        o_ref[one, 1, at : at + k] = real * s + imag * c

    apply_rows(hi_ref, lo_ref, w[3], 1, finish)
    for one in range(j):
        for copy in copies(one):
            copy.start()
    for one in range(j):
        for copy in copies(one):
            copy.wait()


ORDERS = {4: (1, 2, 3, 0), 8: (6, 4, 7, 5, 2, 3, 1, 0)}


def body(amplitudes, gate_blocks, phase_low, phase_high, phase_global):
    cells = amplitudes.shape[1]
    segments, per_segment, _, width, _ = gate_blocks.shape
    spect = cells // (width * width)
    k = SLAB
    v = width // spect // k
    dims = (spect, v, spect, 2, k, width)
    tops = spect * v
    rows = 2 * cells // width
    highs = phase_high.shape[1]
    vmem = pl.BlockSpec(memory_space=pltpu.VMEM)
    anywhere = pl.BlockSpec(memory_space=pl.ANY)
    hbm = pl.BlockSpec(memory_space=pltpu.HBM)
    state_scratch = [pltpu.VMEM(dims, BF16), pltpu.VMEM(dims, BF16)]
    gate_scratch = [
        pltpu.VMEM(gate_blocks.shape[1:], F32),
        pltpu.VMEM((1, segments), F32),
    ]
    in_hbm = functools.partial(pltpu.with_memory_space_constraint, memory_space=pltpu.HBM)
    gates, angles = in_hbm(gate_blocks), in_hbm(
        phase_global.transpose(1, 2, 0).reshape(1, segments)
    )
    params = pltpu.CompilerParams(vmem_limit_bytes=VMEM_LIMIT)

    def cost(scale):
        return pl.CostEstimate(
            flops=int(40 * cells * width * scale),
            bytes_accessed=int(8 * cells * scale),
            transcendentals=0,
        )

    def plan(segment):
        name = "qb" if segment == 1 else "qa"
        count = lax.axis_size(name)
        if count in ORDERS and count <= tops:
            return name, count, name, ORDERS[count]
        return name, count, None, tuple(range(tops))

    def slots_of(order):
        shape = (tops // len(order),) + dims[2:]
        return [jax.ShapeDtypeStruct(shape, F32) for _ in order]

    def exchange(values, segment):
        name, count, mask, order = plan(segment)
        if mask is not None:
            return [
                lax.ppermute(value, name, [(i, i ^ place) for i in range(count)])
                if place
                else value
                for value, place in zip(values, order)
            ]
        value = jnp.concatenate(values, axis=0)
        more = max(count // tops, 1)
        blocks = value.reshape(tops, spect * 2, more, k // more, width)
        blocks = blocks.transpose(0, 2, 1, 3, 4).reshape(count, rows // count, width)
        moved = lax.all_to_all(blocks, name, split_axis=0, concat_axis=0, tiled=True)
        moved = moved.reshape(tops, more, spect * 2, k // more, width)
        moved = moved.transpose(0, 2, 1, 3, 4).reshape((tops, 1) + dims[2:])
        return [moved[i] for i in range(tops)]

    x = amplitudes.reshape(2, cells // width, width).transpose(1, 0, 2).reshape(rows, width)
    name, count, mask, order = plan(0)
    state = pl.pallas_call(
        functools.partial(first_kernel, spect, mask, count, order),
        out_shape=slots_of(order),
        in_specs=[hbm] * 3,
        out_specs=[vmem] * len(order),
        scratch_shapes=state_scratch
        + [pltpu.VMEM((rows, width), F32)]
        + gate_scratch
        + [
            pltpu.VMEM((1, 2, 2 * width, 2 * width), BF16),
            pltpu.SemaphoreType.DMA((per_segment,)),
            pltpu.SemaphoreType.DMA((spect + 1,)),
        ],
        compiler_params=params,
        cost_estimate=cost(1),
    )(in_hbm(x), gates, angles)

    out_dims = (tops * k, spect, 2, width)
    for segment in range(1, segments):
        before = state[-1]
        last = segment == segments - 1
        in_axis, in_count, in_mask, in_order = plan(segment - 1)
        came, goes, out_order = (in_axis, in_count, in_mask), None, None
        if not last:
            out_axis, out_count, out_mask, out_order = plan(segment)
            goes = (out_axis, out_count, out_mask)
        e_shape = (max(v * spect // in_count, 1),) + dims[2:]
        joins = segment % 2 == 1
        w_shape = (6 if joins else 4, 2, 2 * width, 2 * width)
        tables = [w_shape, e_shape] + ([dims] if last else [])
        made = pl.pallas_call(
            functools.partial(prepare_kernel, spect, segment, came, goes, joins),
            out_shape=[
                jax.ShapeDtypeStruct(shape, F32 if n else BF16) for n, shape in enumerate(tables)
            ],
            in_specs=[hbm, hbm, vmem, vmem, anywhere],
            out_specs=[vmem] * len(tables),
            scratch_shapes=gate_scratch
            + [
                pltpu.VMEM((2,) + gate_blocks.shape[2:], F32),
                pltpu.VMEM((highs, width), F32),
                pltpu.VMEM((highs, width), F32),
                pltpu.SemaphoreType.DMA((per_segment,)),
                pltpu.SemaphoreType.DMA((3,)),
            ],
            compiler_params=params,
            cost_estimate=cost(1),
        )(gates, angles, phase_low, phase_high, before)
        state = exchange(state, segment - 1)
        state = pl.pallas_call(
            functools.partial(later_kernel, in_order, out_order, last),
            out_shape=jax.ShapeDtypeStruct(out_dims, F32) if last else slots_of(out_order),
            in_specs=[vmem] * (len(in_order) + len(made)),
            out_specs=hbm if last else [vmem] * len(out_order),
            scratch_shapes=state_scratch
            + (
                [
                    pltpu.VMEM(out_dims[1:3] + (out_dims[0], width), F32),
                    pltpu.SemaphoreType.DMA(out_dims[1:3]),
                ]
                if last
                else []
            ),
            compiler_params=params,
            cost_estimate=cost(1),
        )(*state, *made)
    return state.reshape(cells // width, 2, width).transpose(1, 0, 2).reshape(2, cells)


def solution(mesh):
    return jax.shard_map(
        body,
        mesh=mesh,
        in_specs=(P(None, ("qa", "qb")), P(), P(), P(), P(None, "qa", "qb")),
        out_specs=P(None, ("qa", "qb")),
        check_vma=False,
    )
```

```python
import functools

import jax
import jax.numpy as jnp
from jax import lax
from jax.experimental import pallas as pl
from jax.experimental.pallas import tpu as pltpu
from jax.sharding import PartitionSpec as P

F32 = jnp.float32
BF16 = jnp.bfloat16
SLAB = 16
VMEM_LIMIT = 16 << 20


def split(x):
    high = x.astype(BF16)
    return high, (x - high.astype(F32)).astype(BF16)


def dot(a, b):
    return jnp.dot(a, b, preferred_element_type=F32)


def dot3(ah, al, bh, bl):
    return dot(ah, bh) + (dot(al, bh) + dot(ah, bl))


def block_of(real, imag):
    top = jnp.concatenate([real, -imag], axis=1)
    low = jnp.concatenate([imag, real], axis=1)
    return jnp.concatenate([top, low], axis=0)


def gate_block(real, imag):
    rows, width = real.shape
    full = block_of(real, imag).reshape(2, rows // SLAB, SLAB, 2 * width)
    return jnp.stack([full[0], full[1]], axis=1).reshape(2 * rows, 2 * width)


def inner_order(q, width, spect):
    group = SLAB * spect
    return (q // group) * group + (q % spect) * SLAB + (q % group) // spect


def one_hot(rows, cols, test):
    r = lax.broadcasted_iota(jnp.int32, (rows, cols), 0)
    c = lax.broadcasted_iota(jnp.int32, (rows, cols), 1)
    return jnp.where(test(r, c), 1.0, 0.0).astype(BF16)


def rows_inner(ref, width, spect):
    group = SLAB * spect
    return jnp.concatenate(
        [
            ref[pl.ds(top + j, SLAB, stride=spect), :]
            for j in range(spect)
            for top in range(0, width, group)
        ],
        axis=0,
    )


def move_columns(real, imag, test):
    width = real[0].shape[1]
    right = one_hot(width, width, test)
    moved = dot(jnp.concatenate([*real, *imag], axis=0), right).astype(BF16)
    part = [moved[n * width : (n + 1) * width] for n in range(4)]
    return part[:2], part[2:]


def middle_weight(gate_ref, g, spect, natural=False, flip=0):
    width = gate_ref.shape[-1]
    real = split(rows_inner(gate_ref.at[g, 0], width, spect))
    imag = split(rows_inner(gate_ref.at[g, 1], width, spect))
    if not natural:
        real, imag = move_columns(
            real, imag, lambda r, c: (c ^ flip) == inner_order(r, width, spect)
        )
    return [gate_block(r, i) for r, i in zip(real, imag)]


def upper_weight(gate, cosine=None, sine=None, flip=None):
    real, imag = gate[0], gate[1]
    if cosine is not None:
        real, imag = real * cosine - imag * sine, real * sine + imag * cosine
    real, imag = split(real), split(imag)
    if flip is not None:
        real, imag = move_columns(real, imag, lambda r, c: (c ^ flip) == r)
    return [gate_block(r, i) for r, i in zip(real, imag)]


def compose(first, second):
    width = first[0].shape[-1]
    lh, ll = split(jnp.concatenate([second[0], second[1]], axis=1))
    top = jnp.concatenate([first[0], first[1]], axis=1)
    low = jnp.concatenate([-first[1], first[0]], axis=1)
    rh, rl = split(jnp.concatenate([top, low], axis=0))
    joined = dot3(lh, ll, rh, rl)
    return joined[:, :width], joined[:, width:]


def as_column(row):
    width = row.shape[1]
    return jnp.broadcast_to(row, (width, width)).T


def lower_weight(before, after, lows):
    out = []
    for c, s in lows:
        c, s = as_column(c), as_column(s)
        turned = before[0] * c - before[1] * s, before[0] * s + before[1] * c
        real, imag = compose(turned, after)
        out.append([block_of(r, -i) for r, i in zip(split(real.T), split(imag.T))])
    return out


def put_rows(w_ref, n, pair, group, mask):
    for p, value in enumerate(pair):
        for g in range(value.shape[0] // group):
            start = pl.multiple_of((g ^ mask) * group, group)
            w_ref[n, p, pl.ds(start, group), :] = value[g * group : (g + 1) * group]


def put(w_ref, n, pair):
    w_ref[n, 0] = pair[0]
    w_ref[n, 1] = pair[1]


def rotation(ref, segment, width):
    theta = jnp.broadcast_to(ref[0:1, segment : segment + 1], (1, width))
    return jnp.cos(theta), jnp.sin(theta)


def lower_rows(xh, xl, w):
    y = dot3(xh, xl, w[0], w[1])
    half = y.shape[1] // 2
    return y[:, :half], y[:, half:]


def side_by_side(x):
    *lead, _, k, l = x.shape
    rows = functools.reduce(lambda m, n: m * n, lead, k)
    x = x.reshape(rows // k, 2, k, l)
    return jnp.concatenate([x[:, 0].reshape(rows, l), x[:, 1].reshape(rows, l)], axis=1)


def row_gate(take, w, l):
    first, second = take(0), take(1)
    y = dot3(
        w[0],
        w[1],
        jnp.concatenate([first[0], second[0]], axis=1),
        jnp.concatenate([first[1], second[1]], axis=1),
    )
    return y[:, :l], y[:, l:]


def finish_rows(parts, lead, k, done):
    for a in range(lead[0]):
        for b in range(lead[1]):
            at = (a * lead[1] + b) * 2 * k
            for n, part in enumerate(parts):
                done(n, (a, b), part[at : at + k], part[at + k : at + 2 * k])


def apply_rows(hi_ref, lo_ref, w, axis, done, after=None):
    u, v, j, _, k, l = hi_ref.shape
    count, half = (u, v * j * k) if axis == 0 else (j, u * v * k)

    def column(ref, one):
        part = ref[one] if axis == 0 else ref[:, :, one]
        return jnp.concatenate(
            [part[:, :, 0].reshape(half, l), part[:, :, 1].reshape(half, l)], axis=0
        )

    parts = []
    for at in range(0, count, 2):
        parts += row_gate(lambda n: (column(hi_ref, at + n), column(lo_ref, at + n)), w, l)
        if after is not None:
            finish_rows(parts, (u, v), k, lambda n, *rest: done(at + n, *rest))
            after(at)
            parts = []
    if after is None:
        finish_rows(parts, (j, v) if axis == 0 else (u, v), k, done)


def keeper(hi_ref, lo_ref, axis):
    def keep(one, lead, real, imag):
        at = (one, lead[1], lead[0]) if axis == 0 else (*lead, one)
        for ri, value in ((0, real), (1, imag)):
            high, low = split(value)
            hi_ref[(*at, ri)] = high
            lo_ref[(*at, ri)] = low

    return keep


def mask_of(name, count, dims):
    if name is None:
        return 0
    return lax.axis_index(name) * (dims[0] * dims[1] // count)


def sender(outs, order, dims):
    tops = dims[0] * dims[1]
    few = tops // len(outs)

    def put_out(one, lead, real, imag):
        place = lead[0] * dims[1] + lead[1]
        ref = outs[order.index(place // few)]
        ref[place % few, one, 0] = real
        ref[place % few, one, 1] = imag

    return put_out


def load_gates(gate_hbm, segment, gate_ref, sems, wanted):
    return {
        g: pltpu.make_async_copy(gate_hbm.at[segment, g], gate_ref.at[g], sems.at[g])
        for g in wanted
    }


def first_kernel(spect, name, count, order, x_hbm, gate_hbm, angle_hbm, *rest):
    outs = rest[: len(order)]
    hi_ref, lo_ref, x_ref, gate_ref, angle_ref, w_ref, gate_sem, x_sem = rest[len(order) :]
    u, v, j, _, k, l = hi_ref.shape
    gates = load_gates(gate_hbm, 0, gate_ref, gate_sem, (1, 2, 4, 5))
    block = 2 * v * j * k
    pieces = [
        pltpu.make_async_copy(
            x_hbm.at[pl.ds(a * block, block)], x_ref.at[pl.ds(a * block, block)], x_sem.at[a]
        )
        for a in range(u)
    ]
    angle = pltpu.make_async_copy(angle_hbm, angle_ref, x_sem.at[u])
    for copy in [gates[1], *pieces, gates[2], gates[4], gates[5], angle]:
        copy.start()
    half = block // 2
    keep = keeper(hi_ref, lo_ref, 0)
    for copy in [gates[1], gates[2], gates[4], gates[5], angle, *pieces]:
        copy.wait()
    w = middle_weight(gate_ref, 1, spect, True)

    def column(a):
        real = x_ref[pl.ds(a * block, half, stride=2), :]
        imag = x_ref[pl.ds(a * block + 1, half, stride=2), :]
        return split(jnp.concatenate([real, imag], axis=0))

    parts = []
    for at in range(0, u, 2):
        parts += row_gate(lambda n: column(at + n), w, l)
    finish_rows(parts, (j, v), k, keep)
    w = upper_weight(gate_ref[2])
    apply_rows(hi_ref, lo_ref, w, 1, keeper(hi_ref, lo_ref, 1))
    w = middle_weight(gate_ref, 4, spect)
    apply_rows(hi_ref, lo_ref, w, 0, keep)
    cosine, sine = rotation(angle_ref, 0, l)
    put_rows(
        w_ref, 0, upper_weight(gate_ref[5], cosine, sine), 2 * k, mask_of(name, count, (u, v))
    )
    apply_rows(hi_ref, lo_ref, (w_ref[0, 0], w_ref[0, 1]), 1, sender(outs, order, (u, v)))


def exponentials(high_ref, low_ref, segment, c_ref, s_ref):
    width = c_ref.shape[1]
    for at in range(0, high_ref.shape[1], width):
        row = high_ref[segment : segment + 1, at : at + width]
        c_ref[at : at + width] = as_column(jnp.cos(row))
        s_ref[at : at + width] = as_column(jnp.sin(row))
    low = [low_ref[segment : segment + 1, at : at + width] for at in (0, width)]
    return [(jnp.cos(row), jnp.sin(row)) for row in low]


def fill_table(e_ref, lead, start, kinds, c_ref, s_ref, lows):
    spect, _, k, l = e_ref.shape[-4:]
    for j in range(spect):
        at = pl.ds(start + j // 2, kinds, stride=spect // 2)
        ch = jnp.concatenate([c_ref[at, :]] * (k // kinds), axis=0)
        sh = jnp.concatenate([s_ref[at, :]] * (k // kinds), axis=0)
        if lows is not None:
            cl, sl = lows[j % 2]
            ch, sh = ch * cl - sh * sl, sh * cl + ch * sl
        e_ref[(*lead, j, 0)] = ch
        e_ref[(*lead, j, 1)] = sh


def prepare_kernel(
    spect, segment, came, goes, joins, gate_hbm, angle_hbm, low_ref, high_ref, *rest
):
    last = goes is None
    outs, rest = rest[1 : 3 + last], rest[3 + last :]
    w_ref, e_ref = outs[:2]
    gate_ref, angle_ref, old_ref, c_ref, s_ref, gate_sem, old_sem = rest
    width = gate_ref.shape[-1]
    v = width // spect // SLAB
    tops = (spect, v)
    wanted = (0, 1, 2, 3, 4, 5) if joins else (1, 2, 4, 5)
    copies = list(load_gates(gate_hbm, segment, gate_ref, gate_sem, wanted).values())
    if joins:
        copies += [
            pltpu.make_async_copy(gate_hbm.at[segment - 1, g], old_ref.at[n], old_sem.at[n])
            for n, g in enumerate((0, 3))
        ]
    copies.append(pltpu.make_async_copy(angle_hbm, angle_ref, old_sem.at[2]))
    for copy in copies:
        copy.start()
    axis, count, mask = came
    lows = exponentials(high_ref, low_ref, segment - 1, c_ref, s_ref)
    per = high_ref.shape[1] // count
    start = lax.axis_index(axis) * per
    span = SLAB * spect // 2
    kinds = min(SLAB, per * 2 // spect)
    for n in range(e_ref.shape[0]):
        fill_table(
            e_ref, (n,), start + n * span, kinds, c_ref, s_ref, None if joins else lows
        )
    if last:
        ends = exponentials(high_ref, low_ref, segment, c_ref, s_ref)
        for a in range(spect):
            for b in range(v):
                fill_table(outs[2], (a, b), (a * v + b) * span, SLAB, c_ref, s_ref, ends)
    for copy in copies:
        copy.wait()
    cosine, sine = rotation(angle_ref, segment, width)
    arrives = mask_of(mask, count, tops)
    flip, flip_top = (arrives % v) * (width // v), (arrives // v) * (width // spect)
    put(w_ref, 0, middle_weight(gate_ref, 1, spect, flip=flip))
    put(w_ref, 1, upper_weight(gate_ref[2], flip=flip_top))
    put(w_ref, 2, middle_weight(gate_ref, 4, spect))
    final = upper_weight(gate_ref[5], cosine, sine)
    if last:
        put(w_ref, 3, final)
    else:
        put_rows(w_ref, 3, final, 2 * SLAB, mask_of(goes[2], goes[1], tops))
    if joins:
        before = compose(old_ref[0], old_ref[1])
        after = compose(gate_ref[0], gate_ref[3])
        for n, pair in enumerate(lower_weight(before, after, lows)):
            put(w_ref, 4 + n, pair)


def later_kernel(order, out_order, last, *refs):
    slots, (w_ref, e_ref), rest = refs[: len(order)], refs[len(order) : len(order) + 2], refs[
        len(order) + 2 :
    ]
    if last:
        f_ref, o_hbm, hi_ref, lo_ref, o_ref, o_sem = rest
    else:
        outs, (hi_ref, lo_ref) = rest[:-2], rest[-2:]
    u, v, j, _, k, l = hi_ref.shape
    few = u * v // len(order)
    half = v * j * k
    w = [(w_ref[n, 0], w_ref[n, 1]) for n in range(w_ref.shape[0])]

    def arrived(place):
        ref, n = slots[order.index(place // few)], place % few
        ev = n % e_ref.shape[0]
        c, s = e_ref[ev, :, 0], e_ref[ev, :, 1]
        real, imag = ref[n, :, 0], ref[n, :, 1]
        return real * c - imag * s, real * s + imag * c

    both = [arrived(place) for place in range(u * v)]
    state = [jnp.stack([one[n] for one in both]) for n in range(2)]
    if len(w) > 4:
        lows = []
        for q in range(2):
            flat = [
                x.reshape(u * v, j // 2, 2, k, l)[:, :, q].reshape(u * half // 2, l)
                for x in state
            ]
            part = lower_rows(*split(jnp.concatenate(flat, axis=1)), w[4 + q])
            lows.append([x.reshape(u * v, j // 2, k, l) for x in part])
        state = [jnp.stack([lows[0][n], lows[1][n]], axis=2) for n in range(2)]
    real, imag = (x.reshape(u, half, l) for x in state)

    def column(a):
        return split(jnp.concatenate([real[a], imag[a]], axis=0))

    keep = keeper(hi_ref, lo_ref, 0)
    parts = []
    for at in range(0, u, 2):
        parts += row_gate(lambda n: column(at + n), w[0], l)
    finish_rows(parts, (j, v), k, keep)
    apply_rows(hi_ref, lo_ref, w[1], 1, keeper(hi_ref, lo_ref, 1))
    apply_rows(hi_ref, lo_ref, w[2], 0, keeper(hi_ref, lo_ref, 0))
    if not last:
        apply_rows(hi_ref, lo_ref, w[3], 1, sender(outs, out_order, (u, v)))
        return

    def copies(one):
        return [
            pltpu.make_async_copy(o_ref.at[one, ri], o_hbm.at[:, one, ri], o_sem.at[one, ri])
            for ri in range(2)
        ]

    def finish(one, lead, real, imag):
        c, s = (f_ref[(*lead, one, ri)] for ri in range(2))
        at = (lead[0] * v + lead[1]) * k
        o_ref[one, 0, at : at + k] = real * c - imag * s
        o_ref[one, 1, at : at + k] = real * s + imag * c

    def start(at):
        for copy in copies(at) + copies(at + 1):
            copy.start()

    apply_rows(hi_ref, lo_ref, w[3], 1, finish, start)
    for one in range(j):
        for copy in copies(one):
            copy.wait()


ORDERS = {4: (1, 2, 3, 0), 8: (6, 4, 7, 5, 2, 3, 1, 0)}


def body(amplitudes, gate_blocks, phase_low, phase_high, phase_global):
    cells = amplitudes.shape[1]
    segments, per_segment, _, width, _ = gate_blocks.shape
    spect = cells // (width * width)
    k = SLAB
    v = width // spect // k
    dims = (spect, v, spect, 2, k, width)
    tops = spect * v
    rows = 2 * cells // width
    highs = phase_high.shape[1]
    vmem = pl.BlockSpec(memory_space=pltpu.VMEM)
    anywhere = pl.BlockSpec(memory_space=pl.ANY)
    hbm = pl.BlockSpec(memory_space=pltpu.HBM)
    state_scratch = [pltpu.VMEM(dims, BF16), pltpu.VMEM(dims, BF16)]
    gate_scratch = [
        pltpu.VMEM(gate_blocks.shape[1:], F32),
        pltpu.VMEM((1, segments), F32),
    ]
    in_hbm = functools.partial(pltpu.with_memory_space_constraint, memory_space=pltpu.HBM)
    gates, angles = in_hbm(gate_blocks), in_hbm(
        phase_global.transpose(1, 2, 0).reshape(1, segments)
    )
    params = pltpu.CompilerParams(
        vmem_limit_bytes=VMEM_LIMIT,
    )

    def cost(scale):
        return pl.CostEstimate(
            flops=int(40 * cells * width * scale),
            bytes_accessed=int(8 * cells * scale),
            transcendentals=0,
        )

    def plan(segment):
        name = "qb" if segment == 1 else "qa"
        count = lax.axis_size(name)
        if count in ORDERS and count <= tops:
            return name, count, name, ORDERS[count]
        return name, count, None, tuple(range(tops))

    def slots_of(order):
        shape = (tops // len(order),) + dims[2:]
        return [jax.ShapeDtypeStruct(shape, F32) for _ in order]

    def exchange(values, segment):
        name, count, mask, order = plan(segment)
        if mask is not None:
            return [
                lax.ppermute(value, name, [(i, i ^ place) for i in range(count)])
                if place
                else value
                for value, place in zip(values, order)
            ]
        value = jnp.concatenate(values, axis=0)
        more = max(count // tops, 1)
        blocks = value.reshape(tops, spect * 2, more, k // more, width)
        blocks = blocks.transpose(0, 2, 1, 3, 4).reshape(count, rows // count, width)
        moved = lax.all_to_all(blocks, name, split_axis=0, concat_axis=0, tiled=True)
        moved = moved.reshape(tops, more, spect * 2, k // more, width)
        moved = moved.transpose(0, 2, 1, 3, 4).reshape((tops, 1) + dims[2:])
        return [moved[i] for i in range(tops)]

    x = amplitudes.reshape(2, cells // width, width).transpose(1, 0, 2).reshape(rows, width)
    name, count, mask, order = plan(0)
    state = pl.pallas_call(
        functools.partial(first_kernel, spect, mask, count, order),
        out_shape=slots_of(order),
        in_specs=[hbm] * 3,
        out_specs=[vmem] * len(order),
        scratch_shapes=state_scratch
        + [pltpu.VMEM((rows, width), F32)]
        + gate_scratch
        + [
            pltpu.VMEM((1, 2, 2 * width, 2 * width), BF16),
            pltpu.SemaphoreType.DMA((per_segment,)),
            pltpu.SemaphoreType.DMA((spect + 1,)),
        ],
        compiler_params=params,
        cost_estimate=cost(1),
    )(in_hbm(x), gates, angles)

    out_dims = (tops * k, spect, 2, width)
    for segment in range(1, segments):
        before = state[-1]
        last = segment == segments - 1
        in_axis, in_count, in_mask, in_order = plan(segment - 1)
        came, goes, out_order = (in_axis, in_count, in_mask), None, None
        if not last:
            out_axis, out_count, out_mask, out_order = plan(segment)
            goes = (out_axis, out_count, out_mask)
        e_shape = (max(v * spect // in_count, 1),) + dims[2:]
        joins = segment % 2 == 1
        w_shape = (6 if joins else 4, 2, 2 * width, 2 * width)
        tables = [w_shape, e_shape] + ([dims] if last else [])
        made = pl.pallas_call(
            functools.partial(prepare_kernel, spect, segment, came, goes, joins),
            out_shape=[
                jax.ShapeDtypeStruct(shape, F32 if n else BF16) for n, shape in enumerate(tables)
            ],
            in_specs=[hbm, hbm, vmem, vmem, anywhere],
            out_specs=[vmem] * len(tables),
            scratch_shapes=gate_scratch
            + [
                pltpu.VMEM((2,) + gate_blocks.shape[2:], F32),
                pltpu.VMEM((highs, width), F32),
                pltpu.VMEM((highs, width), F32),
                pltpu.SemaphoreType.DMA((per_segment,)),
                pltpu.SemaphoreType.DMA((3,)),
            ],
            compiler_params=params,
            cost_estimate=cost(1),
        )(gates, angles, phase_low, phase_high, before)
        state = exchange(state, segment - 1)
        state = pl.pallas_call(
            functools.partial(later_kernel, in_order, out_order, last),
            out_shape=jax.ShapeDtypeStruct(out_dims, F32) if last else slots_of(out_order),
            in_specs=[vmem] * (len(in_order) + len(made)),
            out_specs=hbm if last else [vmem] * len(out_order),
            scratch_shapes=state_scratch
            + (
                [
                    pltpu.VMEM(out_dims[1:3] + (out_dims[0], width), F32),
                    pltpu.SemaphoreType.DMA(out_dims[1:3]),
                ]
                if last
                else []
            ),
            compiler_params=params,
            cost_estimate=cost(1),
        )(*state, *made)
    return state.reshape(cells // width, 2, width).transpose(1, 0, 2).reshape(2, cells)


def solution(mesh):
    return jax.shard_map(
        body,
        mesh=mesh,
        in_specs=(P(None, ("qa", "qb")), P(), P(), P(), P(None, "qa", "qb")),
        out_specs=P(None, ("qa", "qb")),
        check_vma=False,
    )
```
